32 devices in a mesh: grp: 2 (over y), ctx: 4 (over z), head: 4 (over x, core).
Axes of the slice: x: 2, y: 2, z: 4, core: 2. Of those that a mesh axis runs over, the one named last changes fastest.
Arguments:
- inputs: bfloat16 [8192, 2560], P(('grp', 'ctx'), 'head'), parts along dimension 0, may hold values from -0.29882812 to 0.29882812
- write_coeffs: bfloat16 [8192, 128], P(('grp', 'ctx')), parts along dimension 0, may hold values from -1.796875 to 1.796875
- read_coeffs: bfloat16 [8192, 128], P(('grp', 'ctx')), parts along dimension 0, may hold values from -1.796875 to 1.796875
- log_decay: float32 [8192, 40], P(('grp', 'ctx'), 'head'), parts along dimension 0, may hold values from -1.6 to 0
- out_grad: bfloat16 [8192, 2560], P(('grp', 'ctx'), 'head'), parts along dimension 0, may hold values from -0.29882812 to 0.29882812
Outputs:
- outputs: bfloat16 [8192, 2560], P(('grp', 'ctx'), 'head'), parts along dimension 0
- in_grad: bfloat16 [8192, 2560], P(('grp', 'ctx'), 'head'), parts along dimension 0
- write_grad: float32 [8192, 128], P(('grp', 'ctx')), parts along dimension 0
- read_grad: float32 [8192, 128], P(('grp', 'ctx')), parts along dimension 0
- decay_grad: float32 [8192, 40], P(('grp', 'ctx'), 'head'), parts along dimension 0
The draws below stay inside these ranges and needn't reach their ends.
There are 2 independent parts, one for each index of `grp`. The reference program is written for one: setup_inputs(seed, part) draws one part's arguments, and reference() takes and returns one part's arrays. A program takes and returns all parts, laid end to end along the dimension named above; each array names one. Nothing has to cross between parts.
All inputs are finite; a program needn't handle non-finite values.
Results may differ from the reference program's by a relative error of at most 0.0071.
Values sent between devices are 32-bit elements; how exact they have to be, the bound alone decides.
A program may use at most 64 MiB of HBM per device.

```python
import jax
import jax.numpy as jnp
from jax import lax

MIXER_HEADS = 40
HEAD_DIM = 64
STATE = 128
BLOCK = 256
TOK_DEV = 1024
SEQUENCE_LENGTH = 4096


def draw_log_decay(key, part):
    random_subkeys = jax.random.split(jax.random.fold_in(key, 11), 7)
    fast_share = 0.5
    is_quick = jax.random.bernoulli(random_subkeys[0], fast_share, (MIXER_HEADS,))
    quick_rate = jax.random.uniform(random_subkeys[1], (MIXER_HEADS,), jnp.float32, 1.0 / 50.0, 1.0 / 30.0)
    slow_rate = jax.random.uniform(random_subkeys[2], (MIXER_HEADS,), jnp.float32, 0.2, 0.5) / SEQUENCE_LENGTH
    step_rates = jnp.where(is_quick, quick_rate, slow_rate)
    roughness = jax.random.uniform(random_subkeys[3], (SEQUENCE_LENGTH // TOK_DEV, TOK_DEV, MIXER_HEADS), jnp.float32, 0.5, 1.5)
    device_factor = jax.random.uniform(random_subkeys[4], (SEQUENCE_LENGTH // TOK_DEV, 1, MIXER_HEADS), jnp.float32, 0.7, 1.4)
    stable_baseline = (roughness * device_factor).reshape(SEQUENCE_LENGTH, MIXER_HEADS) * step_rates[None, :]
    spike_locations = jax.random.randint(random_subkeys[5], (3,), 0, SEQUENCE_LENGTH)
    spike_penalty = jax.random.uniform(random_subkeys[6], (3, MIXER_HEADS), jnp.float32, 0.22, 0.5)
    spike_matches = (jnp.arange(SEQUENCE_LENGTH)[:, None] == spike_locations[None, :]).astype(jnp.float32)
    spike_events = jnp.sum(spike_matches[:, :, None] * spike_penalty[None, :, :], axis=1)
    return -(stable_baseline + spike_events)


def steps_of(stream_key, dims, shards, smallest, high):
    def one(axis_at, shards_of):
        draws = jax.random.uniform(jax.random.fold_in(jax.random.fold_in(stream_key, 6), axis_at), (shards_of,), jnp.float32, smallest / len(shards), high / len(shards))
        return jnp.repeat(jnp.exp(draws), dims[axis_at] // shards_of).reshape((-1,) + (1,) * (len(dims) - axis_at - 1))

    loudness = one(*shards[0])
    for cut in shards[1:]:
        loudness = loudness * one(*cut)
    return loudness


def bell_draw(own_key, shape, deviation, limit, shards=(), held_as=jnp.bfloat16):
    result = jax.random.normal(own_key, shape, jnp.float32) * deviation
    if len(shards) > 0:
        result = steps_of(own_key, shape, shards, -0.22, 0.18) * result
    return jnp.clip(result, min=-limit, max=limit).astype(held_as)


def setup_inputs(seed: int = 0, part: int = 0) -> dict:
    key_list = jax.random.split(jax.random.key(seed), 6)
    own_keys = jax.random.split(jax.random.fold_in(key_list[5], part), 6)
    inputs = bell_draw(own_keys[0], (SEQUENCE_LENGTH, MIXER_HEADS * HEAD_DIM), 0.05, 0.29882812, ((0, 4), (1, 4)))
    write_coeffs = bell_draw(own_keys[1], (SEQUENCE_LENGTH, STATE), 0.3, 1.796875, ((0, 4),))
    read_coeffs = bell_draw(own_keys[2], (SEQUENCE_LENGTH, STATE), 0.3, 1.796875, ((0, 4),))
    log_decay = draw_log_decay(jax.random.fold_in(jax.random.fold_in(key_list[5], part), 71), part)
    out_grad = bell_draw(own_keys[4], (SEQUENCE_LENGTH, MIXER_HEADS * HEAD_DIM), 0.05, 0.29882812, ((0, 4), (1, 4)))
    return dict(inputs=inputs, write_coeffs=write_coeffs, read_coeffs=read_coeffs, log_decay=log_decay, out_grad=out_grad)


def rounded(values):
    return lax.optimization_barrier(values.astype(jnp.bfloat16)).astype(jnp.float32)


def split_blocks(array):
    return array.reshape((SEQUENCE_LENGTH // BLOCK, BLOCK) + array.shape[1:])


def product(form, left, right):
    return jnp.einsum(form, left, right, precision=lax.Precision.HIGHEST)


def inner_terms(pieces):
    inputs, write_c, read_c, running, grads = pieces
    totals = running[-1:, :]
    across = running.T
    spread = across[:, :, None] - across[:, None, :]
    causal = jnp.arange(BLOCK)[:, None] >= jnp.arange(BLOCK)[None, :]
    decays = jnp.where(causal, jnp.exp(jnp.where(causal, spread, 0.0)), 0.0)
    scores = jnp.dot(read_c, write_c.T, preferred_element_type=jnp.float32)
    weights = rounded(scores[None] * decays)
    x_wide = inputs.astype(jnp.float32)
    dy_wide = grads.astype(jnp.float32)
    b_wide = write_c.astype(jnp.float32)
    c_wide = read_c.astype(jnp.float32)
    y_inner = product("hts,shp->thp", weights, x_wide)
    dx_inner = product("hts,thp->shp", weights, dy_wide)
    pairs = product("thp,shp->hts", dy_wide, x_wide)
    pair_weights = rounded(pairs * decays)
    dc_inner = product("hts,sn->tn", pair_weights, b_wide)
    db_inner = product("hts,tn->sn", pair_weights, c_wide)
    grow = jnp.exp(running)[:, :, None]
    shrink = jnp.exp(totals - running)[:, :, None]
    block_state = product("sn,shp->hnp", b_wide, rounded(x_wide * shrink))
    block_adjoint = product("tn,thp->hnp", c_wide, rounded(dy_wide * grow))
    return y_inner, dx_inner, dc_inner, db_inner, block_state, block_adjoint, jnp.exp(totals[0])


def outer_terms(pieces):
    inputs, write_c, read_c, running, grads, state, adjoint = pieces
    totals = running[-1:, :]
    grow = jnp.exp(running)[:, :, None]
    shrink = jnp.exp(totals - running)[:, :, None]
    x_wide = inputs.astype(jnp.float32)
    dy_wide = grads.astype(jnp.float32)
    y_outer = grow * product("tn,hnp->thp", read_c.astype(jnp.float32), state)
    dx_outer = shrink * product("sn,hnp->shp", write_c.astype(jnp.float32), adjoint)
    dc_outer = product("thp,hnp->tn", dy_wide * grow, state)
    db_outer = product("shp,hnp->sn", x_wide * shrink, adjoint)
    return y_outer, dx_outer, dc_outer, db_outer


def reference(inputs, write_coeffs, read_coeffs, log_decay, out_grad):
    x_blocks = split_blocks(inputs.reshape(SEQUENCE_LENGTH, MIXER_HEADS, HEAD_DIM))
    dy_blocks = split_blocks(out_grad.reshape(SEQUENCE_LENGTH, MIXER_HEADS, HEAD_DIM))
    b_blocks = split_blocks(write_coeffs)
    c_blocks = split_blocks(read_coeffs)
    running = jnp.cumsum(split_blocks(log_decay), axis=1)
    y_inner, dx_inner, dc_inner, db_inner, states, adjoints, gains = lax.map(
        inner_terms, (x_blocks, b_blocks, c_blocks, running, dy_blocks))
    empty = jnp.zeros((MIXER_HEADS, STATE, HEAD_DIM), jnp.float32)

    def advance(carry, item):
        gain, piece = item
        return gain[:, None, None] * carry + piece, carry

    _, entering = lax.scan(advance, empty, (gains, states))
    _, leaving = lax.scan(advance, empty, (gains, adjoints), reverse=True)
    y_outer, dx_outer, dc_outer, db_outer = lax.map(
        outer_terms, (x_blocks, b_blocks, c_blocks, running, dy_blocks, entering, leaving))
    y_full = y_inner + y_outer
    dx_full = dx_inner + dx_outer
    read_grad = (dc_inner + dc_outer).reshape(SEQUENCE_LENGTH, STATE)
    write_grad = (db_inner + db_outer).reshape(SEQUENCE_LENGTH, STATE)
    balance = jnp.sum(dy_blocks.astype(jnp.float32) * y_full, axis=-1) - jnp.sum(x_blocks.astype(jnp.float32) * dx_full, axis=-1)
    balance = balance.reshape(SEQUENCE_LENGTH, MIXER_HEADS)
    decay_grad = jnp.flip(jnp.cumsum(jnp.flip(balance, 0), axis=0), 0)
    outputs = y_full.reshape(SEQUENCE_LENGTH, MIXER_HEADS * HEAD_DIM).astype(jnp.bfloat16)
    in_grad = dx_full.reshape(SEQUENCE_LENGTH, MIXER_HEADS * HEAD_DIM).astype(jnp.bfloat16)
    return outputs, in_grad, write_grad, read_grad, decay_grad
```

```python
import functools
import math

import jax
import jax.numpy as jnp
from jax import lax
from jax.experimental import pallas as pl
from jax.experimental.pallas import tpu as pltpu
from jax.sharding import PartitionSpec as P

HEAD_DIM = 64
STATE = 128
BLOCK = 256
LANES = 128
HOP_UNITS = 7
PAIR_TICKS = (0, 2, 4)
EARLY_TICKS = (1, 2)
MIDDLE_TICKS = 1
CHUNKS = 16
SLABS = 4
LOG2E = math.log2(math.e)
F32 = jnp.float32
BF16 = jnp.bfloat16
MESH = pl.DeviceIdType.MESH


def mxu(left, right, contract=((1,), (0,))):
    return lax.dot_general(left, right, (contract, ((), ())), preferred_element_type=F32)


def thirds(values):
    high = values.astype(BF16)
    rest = values - high.astype(F32)
    middle = rest.astype(BF16)
    low = (rest - middle.astype(F32)).astype(BF16)
    return jnp.concatenate([high, middle, low], axis=0)


def iota(shape, dim):
    return lax.broadcasted_iota(jnp.int32, shape, dim)


def mixer_kernel(
    ring, chips, heads, blocks,
    x_hbm, b_hbm, c_hbm, ld_hbm, dy_hbm,
    rounded_out, grads, back_in, dg_ref,
    vec, coef, coef_t, ld_in, ldp, runc, runr, scale, gain, scaled, scaled_t, pieces, states, held,
    dev, inc, out_state, inner, scores, ptotal, left_w, right_w, bal, mate_in, far_in,
    load_sem,
    chain_send, chain_recv, mate_send, mate_recv, far_send, far_recv, back_send, back_recv,
):
    place = lax.axis_index("ctx")
    head = lax.axis_index("head")
    core = lax.rem(head, 2)
    mate = head + 1 - 2 * core
    chip = lax.div(head, 2)
    pairs = heads // 2
    width = heads * HEAD_DIM
    half = BLOCK // 2
    chunk_rows = STATE // CHUNKS
    slab_rows = STATE // SLABS
    part_rows = slab_rows // 2

    loads = [
        pltpu.make_async_copy(ld_hbm, ld_in, load_sem.at[0]),
        pltpu.make_async_copy(c_hbm, coef.at[0], load_sem.at[1]),
        pltpu.make_async_copy(b_hbm, coef.at[1], load_sem.at[2]),
        pltpu.make_async_copy(dy_hbm, vec.at[0], load_sem.at[3]),
        pltpu.make_async_copy(x_hbm, vec.at[1], load_sem.at[4]),
    ]
    for copy in loads:
        copy.start()

    barrier = pltpu.get_barrier_semaphore()
    pl.semaphore_signal(barrier, inc=1, device_id={"head": mate}, device_id_type=MESH)
    for hop in range(1, chips):
        pl.semaphore_signal(
            barrier, inc=1, device_id={"head": lax.rem(head + 2 * hop, 2 * chips)}, device_id_type=MESH
        )

    @pl.when(place > 0)
    def _():
        pl.semaphore_signal(barrier, inc=1, device_id={"ctx": place - 1}, device_id_type=MESH)

    @pl.when(place < ring - 1)
    def _():
        pl.semaphore_signal(barrier, inc=1, device_id={"ctx": place + 1}, device_id_type=MESH)

    slots = ldp.shape[0]
    upper = (iota((BLOCK, BLOCK), 0) <= iota((BLOCK, BLOCK), 1)).astype(F32).astype(BF16)
    spread = (iota((slots, width), 0) == lax.div(iota((slots, width), 1), HEAD_DIM)).astype(F32)
    spread3 = jnp.concatenate([spread] * 3, axis=0).astype(BF16)

    def joined(left3, right):
        three = mxu(left3, right)
        return three[0:slots] + three[slots : 2 * slots] + three[2 * slots :]

    ldp[...] = jnp.zeros_like(ldp)
    loads[0].wait()
    ldp[0:heads, :] = ld_in[...]

    for j in range(blocks):
        rows = slice(j * BLOCK, (j + 1) * BLOCK)
        run = joined(thirds(ldp[:, rows]), upper) * LOG2E
        runr[j] = run
        runc[j] = jnp.concatenate([run, jnp.zeros((LANES - slots, BLOCK), F32)], axis=0).T
        grow = mxu(thirds(jnp.exp2(run)), spread3, ((0,), (0,)))
        scale[0, rows, :] = grow
        scale[1, rows, :] = mxu(
            thirds(jnp.exp2(run[:, BLOCK - 1 :] - run)), spread3, ((0,), (0,))
        )
        gain[j] = jnp.broadcast_to(grow[BLOCK - 1 :, :], (8, width))

    for copy in loads[1:]:
        copy.wait()

    for j in range(blocks):
        for d in range(2):
            rows = slice(j * BLOCK, (j + 1) * BLOCK)
            flipped = coef[d, rows, :].T
            coef_t[d, j] = flipped
            row = (vec[d, rows, :].astype(F32) * scale[d, rows, :]).astype(BF16)
            scaled[d, rows, :] = row
            pieces[1 - d, j] = mxu(flipped, row)

    product = gain[0]
    for j in range(1, blocks):
        product = product * gain[j]
    gain[blocks] = product

    pl.semaphore_wait(barrier, chips + (place > 0).astype(jnp.int32) + (place < ring - 1).astype(jnp.int32))

    first = (2 * place > ring - 1).astype(jnp.int32)
    second = 1 - first

    def hops(d):
        return jnp.where(d == 0, place, ring - 1 - place)

    def chunk(k):
        return pl.ds(pl.multiple_of(k * chunk_rows, chunk_rows), chunk_rows)

    def chain_copy(d, k, source):
        target = jnp.where(d == 0, place + 1, place - 1)
        return pltpu.make_async_remote_copy(
            src_ref=source.at[d, chunk(k)],
            dst_ref=inc.at[d, chunk(k)],
            send_sem=chain_send.at[d, k],
            recv_sem=chain_recv.at[d, k],
            device_id={"ctx": jnp.clip(target, 0, ring - 1)},
            device_id_type=MESH,
        )

    @pl.loop(0, CHUNKS)
    def _(k):
        at = chunk(k)
        forward = pieces[0, 0, at, :]
        backward = pieces[1, blocks - 1, at, :]
        for j in range(1, blocks):
            i = blocks - 1 - j
            forward = gain[j, 0:1, :] * forward + pieces[0, j, at, :]
            backward = gain[i, 0:1, :] * backward + pieces[1, i, at, :]
        dev[0, at] = forward
        dev[1, at] = backward
        for d in range(2):

            @pl.when(hops(d) == 0)
            def _():
                inc[d, at] = jnp.zeros((chunk_rows, width), F32)
                if ring > 1:
                    chain_copy(d, k, dev).start()

    def relay(d, k):
        at = chunk(k)
        chain_copy(d, k, out_state).wait_recv()
        out_state[d, at] = gain[blocks, 0:1, :] * inc[d, at] + dev[d, at]
        chain_copy(d, k, out_state).start()

    def passing(d):
        return (hops(d) > 0) & (hops(d) < ring - 1)

    starts = [(d, jnp.where(passing(d), HOP_UNITS * hops(d), 1 << 20)) for d in (first, second)]

    def tick(unit):
        for d, start in starts:

            @pl.when((unit >= start) & (unit < start + CHUNKS))
            def _():
                relay(d, unit - start)

    def ticked(unit, target):
        last = jnp.maximum(unit, target)

        @pl.loop(unit, last)
        def _(u):
            tick(u)

        return last

    def needed(d, c):
        return jnp.where(passing(d), HOP_UNITS * hops(d) + (c + 1) * (CHUNKS // SLABS), 0)

    def arrive(d, c):
        @pl.when((hops(d) > 0) & (hops(d) == ring - 1))
        def _():
            for k in range(CHUNKS // SLABS):
                chain_copy(d, c * (CHUNKS // SLABS) + k, out_state).wait_recv()

    low_lanes = iota((1, LANES), 1) < HEAD_DIM
    corner = iota((half, half), 0) >= iota((half, half), 1)

    def stacked(x2, at):
        zero = jnp.zeros_like(x2[at])
        return jnp.concatenate(
            [jnp.where(low_lanes, x2[at], zero), jnp.where(low_lanes, zero, x2[at])], axis=0
        )

    early, late = slice(0, half), slice(half, BLOCK)

    @pl.loop(0, blocks)
    def _(j):
        rows = pl.ds(pl.multiple_of(j * BLOCK, BLOCK), BLOCK)
        full = mxu(coef[0, rows, :], coef[1, rows, :], ((1,), (1,)))
        scores[0] = jnp.where(corner, full[early, early], 0.0)
        scores[1] = full[late, early]
        scores[2] = jnp.where(corner, full[late, late], 0.0)
        for p in range(pairs):
            lanes = slice(p * LANES, (p + 1) * LANES)
            x2 = vec[1, rows, lanes]
            dy2 = vec[0, rows, lanes]
            pair_left = mxu(dy2, stacked(x2, early), ((1,), (1,)))
            pair_right = mxu(dy2[late], stacked(x2, late), ((1,), (1,)))
            sums = [None] * 3
            for k in range(2):
                h = 2 * p + k
                side = slice(k * half, (k + 1) * half)
                down = runc[j, :, h : h + 1]
                along = runr[j, h : h + 1, :]
                for q, (t, s) in enumerate(((early, early), (late, early), (late, late))):
                    gap = down[t] - along[:, s]
                    decays = jnp.exp2(gap if q == 1 else jnp.minimum(gap, 0.0))
                    weights = (scores[q] * decays).astype(BF16)
                    if q < 2:
                        left_w[j, p, t, side] = weights
                        pair = pair_left[t, side] * decays
                    else:
                        right_w[j, p, :, side] = weights
                        pair = pair_right[:, side] * decays
                    sums[q] = pair if k == 0 else sums[q] + pair
            for q in range(3):
                if p == 0:
                    ptotal[q] = sums[q]
                else:
                    ptotal[q] += sums[q]
            for d in range(2):
                scaled_t[d, j, lanes, :] = scaled[d, rows, lanes].T
            if p in PAIR_TICKS:
                tick(j * len(PAIR_TICKS) + PAIR_TICKS.index(p))
        top = jnp.where(corner, ptotal[0], 0.0).astype(BF16)
        bottom = jnp.where(corner, ptotal[2], 0.0).astype(BF16)
        both = jnp.concatenate(
            [
                jnp.concatenate([top, jnp.zeros_like(top)], axis=1),
                jnp.concatenate([ptotal[1].astype(BF16), bottom], axis=1),
            ],
            axis=0,
        )
        read_part = mxu(coef_t[1, j], both, ((1,), (1,)))
        write_part = mxu(coef_t[0, j], both)
        for c in range(SLABS):
            for part in range(2):
                at = (2 * c + part) * part_rows
                grads[0, c, part, j] = read_part[at : at + part_rows]
                grads[1, c, part, j] = write_part[at : at + part_rows]

    def inner_rows(j):
        rows = pl.ds(pl.multiple_of(j * BLOCK, BLOCK), BLOCK)
        for p in range(pairs):
            lanes = slice(p * LANES, (p + 1) * LANES)
            x2 = vec[1, rows, lanes]
            flipped = vec[0, rows, lanes].T
            y_left = mxu(left_w[j, p], stacked(x2, early))
            y_right = mxu(right_w[j, p], stacked(x2, late))
            inner[0, rows, lanes] = jnp.concatenate([y_left[early], y_left[late] + y_right], axis=0)
            dx_early = mxu(flipped, left_w[j, p])
            dx_late = mxu(flipped[:, late], right_w[j, p])
            low, high = slice(0, HEAD_DIM), slice(HEAD_DIM, LANES)
            dx2 = jnp.concatenate(
                [
                    jnp.concatenate([dx_early[low, early], dx_late[low, early]], axis=1),
                    jnp.concatenate([dx_early[high, late], dx_late[high, late]], axis=1),
                ],
                axis=0,
            )
            inner[1, rows, lanes] = dx2.T

    def mate_copy(d, c):
        return pltpu.make_async_remote_copy(
            src_ref=grads.at[d, c, 1 - core],
            dst_ref=mate_in.at[d, c],
            send_sem=mate_send.at[d, c],
            recv_sem=mate_recv.at[d, c],
            device_id={"head": mate},
            device_id_type=MESH,
        )

    def far_copy(d, c, hop, source):
        return pltpu.make_async_remote_copy(
            src_ref=mate_in.at[d, c],
            dst_ref=far_in.at[d, c, source],
            send_sem=far_send.at[d, c, hop],
            recv_sem=far_recv.at[d, c, source],
            device_id={"head": lax.rem(head + 2 * hop, 2 * chips)},
            device_id_type=MESH,
        )

    def back_copy(d, c):
        return pltpu.make_async_remote_copy(
            src_ref=grads.at[d, c, core],
            dst_ref=back_in.at[d, c],
            send_sem=back_send.at[d, c],
            recv_sem=back_recv.at[d, c],
            device_id={"head": mate},
            device_id_type=MESH,
        )

    def local_sum(d, c):
        mate_copy(d, c).wait_recv()
        total = mate_in[d, c] + grads[d, c, core]
        mate_in[d, c] = total
        for hop in range(1, chips):
            far_copy(d, c, hop, chip).start()
        far_in[d, c, chip] = total

    def far_sum(d, c):
        for hop in range(1, chips):
            far_copy(d, c, hop, lax.rem(chip + chips - hop, chips)).wait_recv()
        total = far_in[d, c, 0]
        for source in range(1, chips):
            total = total + far_in[d, c, source]
        grads[d, c, core] = total
        back_copy(d, c).start()

    def order(d, i):
        return jnp.where(d == 0, i, blocks - 1 - i)

    def outer_grads(d, c):
        slab = pl.ds(pl.multiple_of(c * slab_rows, slab_rows), slab_rows)
        now = inc[d, slab]
        for i in range(blocks):
            j = order(d, i)
            states[d, j, slab] = now
            now_held = now.astype(BF16)
            held[d, j, slab] = now_held
            add = mxu(now_held, scaled_t[d, j])
            grads[d, c, 0, j] += add[:part_rows]
            grads[d, c, 1, j] += add[part_rows:]
            now = gain[j, 0:1, :] * now + pieces[d, j, slab]
        states[d, blocks, slab] = now
        mate_copy(d, c).start()

    pick = (lax.div(iota((width, LANES), 0), HEAD_DIM) == iota((width, LANES), 1)).astype(F32).astype(BF16)

    def outer_rows(d, j, begins):
        rows = pl.ds(pl.multiple_of(j * BLOCK, BLOCK), BLOCK)
        full = inner[d, rows, :] + scale[d, rows, :] * mxu(coef[d, rows, :], held[d, j])
        rounded_out[d, rows, :] = full.astype(BF16)
        term = vec[d, rows, :].astype(F32) * full
        high = term.astype(BF16)
        low = (term - high.astype(F32)).astype(BF16)
        summed = mxu(high, pick) + mxu(low, pick)
        summed = jnp.where(d == 0, summed, -summed)
        if begins:
            bal[j] = summed
        else:
            bal[j] += summed

    def early_step(i, unit):
        unit = ticked(unit, needed(first, i))
        arrive(first, i)
        outer_grads(first, i)
        unit = ticked(unit, unit + EARLY_TICKS[0])
        inner_rows(i)
        local_sum(first, i)
        return ticked(unit, unit + EARLY_TICKS[1])

    def middle_step(i, unit):
        outer_rows(first, i, True)
        return ticked(unit, unit + MIDDLE_TICKS)

    def late_step(c, unit):
        unit = ticked(unit, needed(second, c))
        arrive(second, c)
        outer_grads(second, c)

        @pl.when(c > 0)
        def _():
            local_sum(second, c - 1)

        return unit

    unit = lax.fori_loop(0, SLABS, early_step, jnp.int32(blocks * len(PAIR_TICKS)))
    unit = lax.fori_loop(0, blocks, middle_step, unit)
    lax.fori_loop(0, SLABS, late_step, unit)

    outer_rows(second, order(second, 0), False)
    local_sum(second, SLABS - 1)

    @pl.loop(1, blocks)
    def _(i):
        outer_rows(second, order(second, i), False)

    @pl.loop(0, SLABS)
    def _(c):
        far_sum(first, c)

    for j in range(blocks):
        joint = jnp.sum(states[0, j + 1] * states[1, j], axis=0, keepdims=True)
        later = jnp.sum(spread * joint, axis=1, keepdims=True)
        lower = (iota((BLOCK, BLOCK), 0) >= iota((BLOCK, BLOCK), 1)).astype(F32).astype(BF16)
        suffix = joined(thirds(bal[j].T[0:slots]), lower) + later
        dg_ref[:, j * BLOCK : (j + 1) * BLOCK] = suffix[0:heads, :]

    @pl.loop(0, SLABS)
    def _(c):
        far_sum(second, c)

    @pl.loop(0, SLABS)
    def _(c):
        for d in range(2):
            back_copy(d, c).wait_recv()
            mate_copy(d, c).wait_send()
            back_copy(d, c).wait_send()
            for hop in range(1, chips):
                far_copy(d, c, hop, chip).wait_send()

    for d in range(2):

        @pl.when(hops(d) < ring - 1)
        def _():
            @pl.loop(0, CHUNKS)
            def _(k):
                chain_copy(d, k, out_state).wait_send()


def store_kernel(rounded_out, grads, back_in, dg_in, y_hbm, dx_hbm, db_hbm, dc_hbm, dg_hbm, turned, sem):
    core = lax.rem(lax.axis_index("head"), 2)
    copies = [
        pltpu.make_async_copy(rounded_out.at[0], y_hbm, sem.at[0]),
        pltpu.make_async_copy(rounded_out.at[1], dx_hbm, sem.at[1]),
        pltpu.make_async_copy(dg_in, dg_hbm, sem.at[2]),
    ]
    for copy in copies:
        copy.start()
    for d, out in ((0, dc_hbm), (1, db_hbm)):
        for j in range(grads.shape[3]):
            parts = []
            for c in range(SLABS):
                own, other = grads[d, c, core, j], back_in[d, c, j]
                parts += [jnp.where(core == 0, own, other), jnp.where(core == 0, other, own)]
            turned[d, j * BLOCK : (j + 1) * BLOCK, :] = jnp.concatenate(parts, axis=0).T
        copies.append(pltpu.make_async_copy(turned.at[d], out, sem.at[3 + d]))
        copies[-1].start()
    for copy in copies:
        copy.wait()


def hbm(array):
    return pltpu.with_memory_space_constraint(array, pltpu.HBM)


def per_device(ring, chips, inputs, write_coeffs, read_coeffs, log_decay, out_grad):
    tokens = inputs.shape[0]
    real = log_decay.shape[1]
    heads = real + real % 2
    if heads > real:
        extra = ((0, 0), (0, (heads - real) * HEAD_DIM))
        inputs = jnp.pad(inputs, extra)
        out_grad = jnp.pad(out_grad, extra)
        log_decay = jnp.pad(log_decay, ((0, 0), (0, heads - real)))
    width = heads * HEAD_DIM
    blocks = tokens // BLOCK
    pairs = heads // 2
    half = BLOCK // 2
    part_rows = STATE // SLABS // 2
    slots = -(-heads // 16) * 16
    any_spec = pl.BlockSpec(memory_space=pl.ANY)
    hbm_spec = pl.BlockSpec(memory_space=pltpu.HBM)
    vmem_spec = pl.BlockSpec(memory_space=pltpu.VMEM)
    dma = pltpu.SemaphoreType.DMA
    results = pl.pallas_call(
        functools.partial(mixer_kernel, ring, chips, heads, blocks),
        out_shape=(
            pltpu.VMEM((2, tokens, width), BF16),
            pltpu.VMEM((2, SLABS, 2, blocks, part_rows, BLOCK), F32),
            pltpu.VMEM((2, SLABS, blocks, part_rows, BLOCK), F32),
            pltpu.VMEM((heads, tokens), F32),
        ),
        in_specs=[hbm_spec] * 5,
        out_specs=(vmem_spec,) * 4,
        scratch_shapes=[
            pltpu.VMEM((2, tokens, width), BF16),
            pltpu.VMEM((2, tokens, STATE), BF16),
            pltpu.VMEM((2, blocks, STATE, BLOCK), BF16),
            pltpu.VMEM((heads, tokens), F32),
            pltpu.VMEM((slots, tokens), F32),
            pltpu.VMEM((blocks, BLOCK, LANES), F32),
            pltpu.VMEM((blocks, slots, BLOCK), F32),
            pltpu.VMEM((2, tokens, width), F32),
            pltpu.VMEM((blocks + 1, 8, width), F32),
            pltpu.VMEM((2, tokens, width), BF16),
            pltpu.VMEM((2, blocks, width, BLOCK), BF16),
            pltpu.VMEM((2, blocks, STATE, width), F32),
            pltpu.VMEM((2, blocks + 1, STATE, width), F32),
            pltpu.VMEM((2, blocks, STATE, width), BF16),
            pltpu.VMEM((2, STATE, width), F32),
            pltpu.VMEM((2, STATE, width), F32),
            pltpu.VMEM((2, STATE, width), F32),
            pltpu.VMEM((2, tokens, width), F32),
            pltpu.VMEM((3, half, half), F32),
            pltpu.VMEM((3, half, half), F32),
            pltpu.VMEM((blocks, pairs, BLOCK, BLOCK), BF16),
            pltpu.VMEM((blocks, pairs, half, BLOCK), BF16),
            pltpu.VMEM((blocks, BLOCK, LANES), F32),
            pltpu.VMEM((2, SLABS, blocks, part_rows, BLOCK), F32),
            pltpu.VMEM((2, SLABS, chips, blocks, part_rows, BLOCK), F32),
            dma((5,)),
            dma((2, CHUNKS)),
            dma((2, CHUNKS)),
            dma((2, SLABS)),
            dma((2, SLABS)),
            dma((2, SLABS, chips)),
            dma((2, SLABS, chips)),
            dma((2, SLABS)),
            dma((2, SLABS)),
        ],
        compiler_params=pltpu.CompilerParams(
            collective_id=0, has_side_effects=True, vmem_limit_bytes=46 * 1024 * 1024
        ),
    )(hbm(inputs), hbm(write_coeffs), hbm(read_coeffs), hbm(log_decay.T), hbm(out_grad))
    y, dx, db, dc, dg = pl.pallas_call(
        store_kernel,
        out_shape=(
            jax.ShapeDtypeStruct((tokens, width), BF16),
            jax.ShapeDtypeStruct((tokens, width), BF16),
            jax.ShapeDtypeStruct((tokens, STATE), F32),
            jax.ShapeDtypeStruct((tokens, STATE), F32),
            jax.ShapeDtypeStruct((heads, tokens), F32),
        ),
        in_specs=[vmem_spec] * 4,
        out_specs=(any_spec,) * 5,
        scratch_shapes=[pltpu.VMEM((2, tokens, STATE), F32), dma((5,))],
        compiler_params=pltpu.CompilerParams(vmem_limit_bytes=8 * 1024 * 1024),
    )(*[pltpu.with_memory_space_constraint(piece, pltpu.VMEM) for piece in results])
    dg = dg.T
    if heads > real:
        y = y[:, : real * HEAD_DIM]
        dx = dx[:, : real * HEAD_DIM]
        dg = dg[:, :real]
    return (y, dx, db, dc, dg)


def solution(mesh):
    in_specs = (
        P(("grp", "ctx"), "head"),
        P(("grp", "ctx"), None),
        P(("grp", "ctx"), None),
        P(("grp", "ctx"), "head"),
        P(("grp", "ctx"), "head"),
    )
    out_specs = (
        P(("grp", "ctx"), "head"),
        P(("grp", "ctx"), "head"),
        P(("grp", "ctx"), None),
        P(("grp", "ctx"), None),
        P(("grp", "ctx"), "head"),
    )
    return jax.shard_map(
        functools.partial(per_device, mesh.shape["ctx"], mesh.shape["head"] // 2),
        mesh=mesh,
        in_specs=in_specs,
        out_specs=out_specs,
        check_vma=False,
    )
```

```python
import functools
import math

import jax
import jax.numpy as jnp
from jax import lax
from jax.experimental import pallas as pl
from jax.experimental.pallas import tpu as pltpu
from jax.sharding import PartitionSpec as P

HEAD_DIM = 64
STATE = 128
BLOCK = 256
LANES = 128
FIRST_UNITS = 2
HOP_UNITS = 4
PAIR_TICKS = (4,)
EARLY_TICKS = (1, 0)
MIDDLE_TICKS = 1
CHUNKS = 8
SLABS = 4
STORES = 1
LOG2E = math.log2(math.e)
F32 = jnp.float32
BF16 = jnp.bfloat16
MESH = pl.DeviceIdType.MESH


def mxu(left, right, contract=((1,), (0,))):
    return lax.dot_general(left, right, (contract, ((), ())), preferred_element_type=F32)


def thirds(values):
    high = values.astype(BF16)
    rest = values - high.astype(F32)
    middle = rest.astype(BF16)
    low = (rest - middle.astype(F32)).astype(BF16)
    return jnp.concatenate([high, middle, low], axis=0)


def iota(shape, dim):
    return lax.broadcasted_iota(jnp.int32, shape, dim)


def mixer_kernel(
    ring, chips, heads, blocks,
    x_hbm, b_hbm, c_hbm, ld_hbm, dy_hbm,
    rounded_out, grads, back_in, dg_ref,
    vec, coef, coef_t, ld_in, ldp, runc, runr, scale, gain, scaled, scaled_t, pieces, states, held,
    dev, inc, out_state, inner, scores, ptotal, left_w, right_w, bal, mate_in, far_in,
    load_sem,
    chain_send, chain_recv, mate_send, mate_recv, far_send, far_recv, back_send, back_recv,
):
    place = lax.axis_index("ctx")
    head = lax.axis_index("head")
    core = lax.rem(head, 2)
    mate = head + 1 - 2 * core
    chip = lax.div(head, 2)
    pairs = heads // 2
    width = heads * HEAD_DIM
    half = BLOCK // 2
    chunk_rows = STATE // CHUNKS
    slab_rows = STATE // SLABS
    part_rows = slab_rows // 2

    first = (2 * place > ring - 1).astype(jnp.int32)
    second = 1 - first

    loads = [
        pltpu.make_async_copy(ld_hbm, ld_in, load_sem.at[0]),
        pltpu.make_async_copy(c_hbm, coef.at[0], load_sem.at[1]),
        pltpu.make_async_copy(b_hbm, coef.at[1], load_sem.at[2]),
        pltpu.make_async_copy(dy_hbm, vec.at[0], load_sem.at[3]),
        pltpu.make_async_copy(x_hbm, vec.at[1], load_sem.at[4]),
    ]
    loads[0].start()

    @pl.when(first == 0)
    def _():
        for n in (2, 4, 1, 3):
            loads[n].start()

    @pl.when(first == 1)
    def _():
        for n in (1, 3, 2, 4):
            loads[n].start()

    def loaded(v):
        for rest in (coef, vec):
            whole = rest.at[v]
            offset = 1 if rest is coef else 3
            pltpu.make_async_copy(whole, whole, load_sem.at[offset + v]).wait()

    barrier = pltpu.get_barrier_semaphore()
    pl.semaphore_signal(barrier, inc=1, device_id={"head": mate}, device_id_type=MESH)
    for hop in range(1, chips):
        pl.semaphore_signal(
            barrier, inc=1, device_id={"head": lax.rem(head + 2 * hop, 2 * chips)}, device_id_type=MESH
        )

    @pl.when(place > 0)
    def _():
        pl.semaphore_signal(barrier, inc=1, device_id={"ctx": place - 1}, device_id_type=MESH)

    @pl.when(place < ring - 1)
    def _():
        pl.semaphore_signal(barrier, inc=1, device_id={"ctx": place + 1}, device_id_type=MESH)

    slots = ldp.shape[0]
    upper = (iota((BLOCK, BLOCK), 0) <= iota((BLOCK, BLOCK), 1)).astype(F32).astype(BF16)
    spread = (iota((slots, width), 0) == lax.div(iota((slots, width), 1), HEAD_DIM)).astype(F32)
    spread3 = jnp.concatenate([spread] * 3, axis=0).astype(BF16)

    def joined(left3, right):
        three = mxu(left3, right)
        return three[0:slots] + three[slots : 2 * slots] + three[2 * slots :]

    ldp[...] = jnp.zeros_like(ldp)
    loads[0].wait()
    ldp[0:heads, :] = ld_in[...]

    def expanded(values):
        return mxu(thirds(jnp.exp2(values)), spread3, ((0,), (0,)))

    def scaled_pieces(v):
        for j in range(blocks):
            run = runr[j]
            rows = slice(j * BLOCK, (j + 1) * BLOCK)
            scale[v, rows, :] = expanded(jnp.where(v == 0, run, run[:, BLOCK - 1 :] - run))
        loaded(v)
        for j in range(blocks):
            rows = slice(j * BLOCK, (j + 1) * BLOCK)
            flipped = coef[v, rows, :].T
            coef_t[v, j] = flipped
            row = (vec[v, rows, :].astype(F32) * scale[v, rows, :]).astype(BF16)
            scaled[v, rows, :] = row
            pieces[1 - v, j] = mxu(flipped, row)

    for j in range(blocks):
        rows = slice(j * BLOCK, (j + 1) * BLOCK)
        run = joined(thirds(ldp[:, rows]), upper) * LOG2E
        runr[j] = run
        gain[j] = expanded(jnp.broadcast_to(run[:, BLOCK - 1 :], (slots, 8)))

    scaled_pieces(second)

    product = gain[0]
    for j in range(1, blocks):
        product = product * gain[j]
    gain[blocks] = product

    pl.semaphore_wait(barrier, chips + (place > 0).astype(jnp.int32) + (place < ring - 1).astype(jnp.int32))

    def hops(d):
        return jnp.where(d == 0, place, ring - 1 - place)

    def chunk(k):
        return pl.ds(pl.multiple_of(k * chunk_rows, chunk_rows), chunk_rows)

    class Null:
        def start(self): pass
        def wait_recv(self): pass
        def wait_send(self): pass

    class Null:
        def start(self): pass
        def wait_recv(self): pass
        def wait_send(self): pass

    class Null:
        def start(self): pass
        def wait_recv(self): pass
        def wait_send(self): pass

    def chain_copy(d, k, source):
        target = jnp.where(d == 0, place + 1, place - 1)
        return pltpu.make_async_remote_copy(
            src_ref=source.at[d, chunk(k)],
            dst_ref=inc.at[d, chunk(k)],
            send_sem=chain_send.at[d],
            recv_sem=chain_recv.at[d, k],
            device_id={"ctx": jnp.clip(target, 0, ring - 1)},
            device_id_type=MESH,
        )

    def device_state(d, sends):
        @pl.loop(0, CHUNKS)
        def _(k):
            at = chunk(k)
            state = pieces[d, jnp.where(d == 0, 0, blocks - 1), at, :]
            for i in range(1, blocks):
                j = jnp.where(d == 0, i, blocks - 1 - i)
                state = gain[j, 0:1, :] * state + pieces[d, j, at, :]
            dev[d, at] = state
            if sends:

                @pl.when(hops(d) == 0)
                def _():
                    inc[d, at] = jnp.zeros((chunk_rows, width), F32)
                    if ring > 1:
                        chain_copy(d, k, dev).start()

    device_state(first, True)
    scaled_pieces(first)
    for j in range(blocks):
        runc[j] = jnp.concatenate([runr[j], jnp.zeros((LANES - slots, BLOCK), F32)], axis=0).T
    device_state(second, ring == 1)

    def relay(d, k):
        at = chunk(k)
        chain_copy(d, k, out_state).wait_recv()
        out_state[d, at] = gain[blocks, 0:1, :] * inc[d, at] + dev[d, at]
        chain_copy(d, k, out_state).start()

    def passing(d):
        return (hops(d) > 0) & (hops(d) < ring - 1)

    starts = [(d, jnp.where(passing(d), (FIRST_UNITS + HOP_UNITS * (hops(d) - 1)), 1 << 20)) for d in (first, second)]

    def tick(unit):
        for d, start in starts:

            @pl.when((unit >= start) & (unit < start + CHUNKS))
            def _():
                relay(d, unit - start)

    def ticked(unit, target):
        last = jnp.maximum(unit, target)

        @pl.loop(unit, last)
        def _(u):
            tick(u)

        return last

    per_slab = CHUNKS // SLABS

    def needed(d, count):
        return jnp.where(passing(d), (FIRST_UNITS + HOP_UNITS * (hops(d) - 1)) + count, 0)

    def arrive(d, k, count):
        @pl.when((hops(d) > 0) & (hops(d) == ring - 1))
        def _():
            for n in range(count):
                chain_copy(d, k + n, out_state).wait_recv()

    low_lanes = iota((1, LANES), 1) < HEAD_DIM
    corner = iota((half, half), 0) >= iota((half, half), 1)

    def stacked(x2, at):
        zero = jnp.zeros_like(x2[at])
        return jnp.concatenate(
            [jnp.where(low_lanes, x2[at], zero), jnp.where(low_lanes, zero, x2[at])], axis=0
        )

    early, late = slice(0, half), slice(half, BLOCK)

    @pl.loop(0, blocks)
    def _(j):
        rows = pl.ds(pl.multiple_of(j * BLOCK, BLOCK), BLOCK)
        full = mxu(coef[0, rows, :], coef[1, rows, :], ((1,), (1,)))
        scores[0] = jnp.where(corner, full[early, early], 0.0)
        scores[1] = full[late, early]
        scores[2] = jnp.where(corner, full[late, late], 0.0)
        for p in range(pairs):
            lanes = slice(p * LANES, (p + 1) * LANES)
            x2 = vec[1, rows, lanes]
            dy2 = vec[0, rows, lanes]
            pair_left = mxu(dy2, stacked(x2, early), ((1,), (1,)))
            pair_right = mxu(dy2[late], stacked(x2, late), ((1,), (1,)))
            sums = [None] * 3
            for k in range(2):
                h = 2 * p + k
                side = slice(k * half, (k + 1) * half)
                down = runc[j, :, h : h + 1]
                along = runr[j, h : h + 1, :]
                for q, (t, s) in enumerate(((early, early), (late, early), (late, late))):
                    gap = down[t] - along[:, s]
                    decays = jnp.exp2(gap if q == 1 else jnp.minimum(gap, 0.0))
                    weights = (scores[q] * decays).astype(BF16)
                    if q < 2:
                        left_w[j, p, t, side] = weights
                        pair = pair_left[t, side] * decays
                    else:
                        right_w[j, p, :, side] = weights
                        pair = pair_right[:, side] * decays
                    sums[q] = pair if k == 0 else sums[q] + pair
            for q in range(3):
                if p == 0:
                    ptotal[q] = sums[q]
                else:
                    ptotal[q] += sums[q]
            for d in range(2):
                scaled_t[d, j, lanes, :] = scaled[d, rows, lanes].T
            if p in PAIR_TICKS:
                tick(j * len(PAIR_TICKS) + PAIR_TICKS.index(p))
        top = jnp.where(corner, ptotal[0], 0.0).astype(BF16)
        bottom = jnp.where(corner, ptotal[2], 0.0).astype(BF16)
        both = jnp.concatenate(
            [
                jnp.concatenate([top, jnp.zeros_like(top)], axis=1),
                jnp.concatenate([ptotal[1].astype(BF16), bottom], axis=1),
            ],
            axis=0,
        )
        read_part = mxu(coef_t[1, j], both, ((1,), (1,)))
        write_part = mxu(coef_t[0, j], both)
        for c in range(SLABS):
            for part in range(2):
                at = (2 * c + part) * part_rows
                grads[0, c, part, j] = read_part[at : at + part_rows]
                grads[1, c, part, j] = write_part[at : at + part_rows]

    def inner_rows(j):
        rows = pl.ds(pl.multiple_of(j * BLOCK, BLOCK), BLOCK)
        for p in range(pairs):
            lanes = slice(p * LANES, (p + 1) * LANES)
            x2 = vec[1, rows, lanes]
            flipped = vec[0, rows, lanes].T
            y_left = mxu(left_w[j, p], stacked(x2, early))
            y_right = mxu(right_w[j, p], stacked(x2, late))
            inner[0, rows, lanes] = jnp.concatenate([y_left[early], y_left[late] + y_right], axis=0)
            dx_early = mxu(flipped, left_w[j, p])
            dx_late = mxu(flipped[:, late], right_w[j, p])
            low, high = slice(0, HEAD_DIM), slice(HEAD_DIM, LANES)
            dx2 = jnp.concatenate(
                [
                    jnp.concatenate([dx_early[low, early], dx_late[low, early]], axis=1),
                    jnp.concatenate([dx_early[high, late], dx_late[high, late]], axis=1),
                ],
                axis=0,
            )
            inner[1, rows, lanes] = dx2.T

    def mate_copy(d, c):
        return pltpu.make_async_remote_copy(
            src_ref=grads.at[d, c, 1 - core],
            dst_ref=mate_in.at[d, c],
            send_sem=mate_send.at[d],
            recv_sem=mate_recv.at[d, c],
            device_id={"head": mate},
            device_id_type=MESH,
        )

    def far_copy(d, c, hop, source):
        return pltpu.make_async_remote_copy(
            src_ref=mate_in.at[d, c],
            dst_ref=far_in.at[d, c, source],
            send_sem=far_send.at[d, hop],
            recv_sem=far_recv.at[d, c, source],
            device_id={"head": lax.rem(head + 2 * hop, 2 * chips)},
            device_id_type=MESH,
        )

    def back_copy(d, c):
        return pltpu.make_async_remote_copy(
            src_ref=grads.at[d, c, core],
            dst_ref=back_in.at[d, c],
            send_sem=back_send.at[d],
            recv_sem=back_recv.at[d],
            device_id={"head": mate},
            device_id_type=MESH,
        )

    def local_sum(d, c):
        mate_copy(d, c).wait_recv()
        total = mate_in[d, c] + grads[d, c, core]
        mate_in[d, c] = total
        for hop in range(1, chips):
            far_copy(d, c, hop, chip).start()
        far_in[d, c, chip] = total

    def far_sum(d, c):
        for hop in range(1, chips):
            far_copy(d, c, hop, lax.rem(chip + chips - hop, chips)).wait_recv()
        total = far_in[d, c, 0]
        for source in range(1, chips):
            total = total + far_in[d, c, source]
        grads[d, c, core] = total
        back_copy(d, c).start()

    def order(d, i):
        return jnp.where(d == 0, i, blocks - 1 - i)

    def outer_part(d, c, offset, count):
        slab = pl.ds(pl.multiple_of(c * slab_rows + offset, part_rows), count)
        now = inc[d, slab]
        for i in range(blocks):
            j = order(d, i)
            states[d, j, slab] = now
            now_held = now.astype(BF16)
            held[d, j, slab] = now_held
            add = mxu(now_held, scaled_t[d, j])
            for n in range(count // part_rows):
                part = offset // part_rows + n
                grads[d, c, part, j] += add[n * part_rows : (n + 1) * part_rows]
            now = gain[j, 0:1, :] * now + pieces[d, j, slab]
        states[d, blocks, slab] = now

    def outer_grads(d, c):
        outer_part(d, c, 0, slab_rows)
        mate_copy(d, c).start()

    pick = (lax.div(iota((width, LANES), 0), HEAD_DIM) == iota((width, LANES), 1)).astype(F32).astype(BF16)

    def outer_rows(d, j, begins):
        other = 1 - d
        rows = pl.ds(pl.multiple_of(j * BLOCK, BLOCK), BLOCK)
        full = inner[d, rows, :] + scale[d, rows, :] * mxu(coef[d, rows, :], held[d, j])
        rounded_out[d, rows, :] = full.astype(BF16)
        term = vec[d, rows, :].astype(F32) * full
        if begins:
            inner[d, rows, :] = term
            return
        term = term - inner[other, rows, :]
        high = term.astype(BF16)
        low = (term - high.astype(F32)).astype(BF16)
        summed = mxu(high, pick) + mxu(low, pick)
        bal[j] = jnp.where(d == 0, summed, -summed)

    def early_step(i, unit):
        unit = ticked(unit, needed(first, (i + 1) * per_slab))
        arrive(first, i * per_slab, per_slab)
        outer_grads(first, i)
        unit = ticked(unit, unit + EARLY_TICKS[0])
        inner_rows(i)
        local_sum(first, i)
        return ticked(unit, unit + EARLY_TICKS[1])

    def middle_step(i, unit):
        outer_rows(first, i, True)
        return ticked(unit, unit + MIDDLE_TICKS)

    def late_step(c, unit):
        unit = ticked(unit, needed(second, (c + 1) * per_slab))
        arrive(second, c * per_slab, per_slab)
        outer_grads(second, c)

        @pl.when(c > 0)
        def _():
            local_sum(second, c - 1)

        return unit

    unit = lax.fori_loop(0, SLABS, early_step, jnp.int32(blocks * len(PAIR_TICKS)))
    unit = lax.fori_loop(0, blocks, middle_step, unit)
    unit = lax.fori_loop(0, SLABS - 1, late_step, unit)
    final = SLABS - 1
    for part in range(2):
        begin = final * per_slab + part * (per_slab // 2)
        unit = ticked(unit, needed(second, begin + per_slab // 2))
        arrive(second, begin, per_slab // 2)
        outer_part(second, final, part * part_rows, part_rows)

        @pl.when(core == 1 - part)
        def _():
            mate_copy(second, final).start()

        if part == 0:
            local_sum(second, final - 1)

    @pl.when(core == 0)
    def _():
        local_sum(second, final)

    outer_rows(second, order(second, 0), False)

    @pl.when(core == 1)
    def _():
        local_sum(second, final)

    @pl.loop(1, blocks)
    def _(i):
        outer_rows(second, order(second, i), False)

    @pl.loop(0, SLABS)
    def _(c):
        far_sum(first, c)

    for j in range(blocks):
        joint = jnp.sum(states[0, j + 1] * states[1, j], axis=0, keepdims=True)
        later = jnp.sum(spread * joint, axis=1, keepdims=True)
        lower = (iota((BLOCK, BLOCK), 0) >= iota((BLOCK, BLOCK), 1)).astype(F32).astype(BF16)
        suffix = joined(thirds(bal[j].T[0:slots]), lower) + later
        dg_ref[:, j * BLOCK : (j + 1) * BLOCK] = suffix[0:heads, :]

    @pl.loop(0, SLABS)
    def _(c):
        far_sum(second, c)

    def whole(d, source, target, send, recv):
        return pltpu.make_async_remote_copy(
            src_ref=source.at[d],
            dst_ref=target.at[d],
            send_sem=send,
            recv_sem=recv,
            device_id={"head": mate},
            device_id_type=MESH,
        )

    for d in range(2):
        everything = whole(d, mate_in, back_in, back_send.at[d], back_recv.at[d])
        everything.wait_recv()
        everything.wait_send()
        whole(d, mate_in, back_in, mate_send.at[d], back_recv.at[d]).wait_send()
        for hop in range(1, chips):
            whole(d, mate_in, back_in, far_send.at[d, hop], back_recv.at[d]).wait_send()

        @pl.when(hops(d) < ring - 1)
        def _():
            whole(d, out_state, inc, chain_send.at[d], back_recv.at[d]).wait_send()


def store_kernel(rounded_out, grads, back_in, dg_in, y_hbm, dx_hbm, db_hbm, dc_hbm, dg_hbm, turned, sem):
    core = lax.rem(lax.axis_index("head"), 2)
    copies = [pltpu.make_async_copy(dg_in, dg_hbm, sem.at[0])]
    tokens = rounded_out.shape[1]
    for part in range(STORES):
        rows = pl.ds(part * (tokens // STORES), tokens // STORES)
        for d, out in ((0, y_hbm), (1, dx_hbm)):
            copies.append(
                pltpu.make_async_copy(rounded_out.at[d, rows], out.at[rows], sem.at[len(copies)])
            )
    for copy in copies:
        copy.start()
    for d, out in ((0, dc_hbm), (1, db_hbm)):
        for j in range(grads.shape[3]):
            parts = []
            for c in range(SLABS):
                own, other = grads[d, c, core, j], back_in[d, c, j]
                parts += [jnp.where(core == 0, own, other), jnp.where(core == 0, other, own)]
            turned[d, j * BLOCK : (j + 1) * BLOCK, :] = jnp.concatenate(parts, axis=0).T
        copies.append(pltpu.make_async_copy(turned.at[d], out, sem.at[len(copies)]))
        copies[-1].start()
    for copy in copies:
        copy.wait()


def hbm(array):
    return pltpu.with_memory_space_constraint(array, pltpu.HBM)


def per_device(ring, chips, inputs, write_coeffs, read_coeffs, log_decay, out_grad):
    tokens = inputs.shape[0]
    real = log_decay.shape[1]
    heads = real + real % 2
    if heads > real:
        extra = ((0, 0), (0, (heads - real) * HEAD_DIM))
        inputs = jnp.pad(inputs, extra)
        out_grad = jnp.pad(out_grad, extra)
        log_decay = jnp.pad(log_decay, ((0, 0), (0, heads - real)))
    width = heads * HEAD_DIM
    blocks = tokens // BLOCK
    pairs = heads // 2
    half = BLOCK // 2
    part_rows = STATE // SLABS // 2
    slots = -(-heads // 16) * 16
    any_spec = pl.BlockSpec(memory_space=pl.ANY)
    hbm_spec = pl.BlockSpec(memory_space=pltpu.HBM)
    vmem_spec = pl.BlockSpec(memory_space=pltpu.VMEM)
    dma = pltpu.SemaphoreType.DMA
    results = pl.pallas_call(
        functools.partial(mixer_kernel, ring, chips, heads, blocks),
        out_shape=(
            pltpu.VMEM((2, tokens, width), BF16),
            pltpu.VMEM((2, SLABS, 2, blocks, part_rows, BLOCK), F32),
            pltpu.VMEM((2, SLABS, blocks, part_rows, BLOCK), F32),
            pltpu.VMEM((heads, tokens), F32),
        ),
        in_specs=[hbm_spec] * 5,
        out_specs=(vmem_spec,) * 4,
        scratch_shapes=[
            pltpu.VMEM((2, tokens, width), BF16),
            pltpu.VMEM((2, tokens, STATE), BF16),
            pltpu.VMEM((2, blocks, STATE, BLOCK), BF16),
            pltpu.VMEM((heads, tokens), F32),
            pltpu.VMEM((slots, tokens), F32),
            pltpu.VMEM((blocks, BLOCK, LANES), F32),
            pltpu.VMEM((blocks, slots, BLOCK), F32),
            pltpu.VMEM((2, tokens, width), F32),
            pltpu.VMEM((blocks + 1, 8, width), F32),
            pltpu.VMEM((2, tokens, width), BF16),
            pltpu.VMEM((2, blocks, width, BLOCK), BF16),
            pltpu.VMEM((2, blocks, STATE, width), F32),
            pltpu.VMEM((2, blocks + 1, STATE, width), F32),
            pltpu.VMEM((2, blocks, STATE, width), BF16),
            pltpu.VMEM((2, STATE, width), F32),
            pltpu.VMEM((2, STATE, width), F32),
            pltpu.VMEM((2, STATE, width), F32),
            pltpu.VMEM((2, tokens, width), F32),
            pltpu.VMEM((3, half, half), F32),
            pltpu.VMEM((3, half, half), F32),
            pltpu.VMEM((blocks, pairs, BLOCK, BLOCK), BF16),
            pltpu.VMEM((blocks, pairs, half, BLOCK), BF16),
            pltpu.VMEM((blocks, BLOCK, LANES), F32),
            pltpu.VMEM((2, SLABS, blocks, part_rows, BLOCK), F32),
            pltpu.VMEM((2, SLABS, chips, blocks, part_rows, BLOCK), F32),
            dma((5,)),
            dma((2,)),
            dma((2, CHUNKS)),
            dma((2,)),
            dma((2, SLABS)),
            dma((2, chips)),
            dma((2, SLABS, chips)),
            dma((2,)),
            dma((2,)),
        ],
        compiler_params=pltpu.CompilerParams(
            collective_id=0, has_side_effects=True, vmem_limit_bytes=46 * 1024 * 1024
        ),
    )(hbm(inputs), hbm(write_coeffs), hbm(read_coeffs), hbm(log_decay.T), hbm(out_grad))
    y, dx, db, dc, dg = pl.pallas_call(
        store_kernel,
        out_shape=(
            jax.ShapeDtypeStruct((tokens, width), BF16),
            jax.ShapeDtypeStruct((tokens, width), BF16),
            jax.ShapeDtypeStruct((tokens, STATE), F32),
            jax.ShapeDtypeStruct((tokens, STATE), F32),
            jax.ShapeDtypeStruct((heads, tokens), F32),
        ),
        in_specs=[vmem_spec] * 4,
        out_specs=(any_spec,) * 5,
        scratch_shapes=[pltpu.VMEM((2, tokens, STATE), F32), dma((3 + 2 * STORES,))],
        compiler_params=pltpu.CompilerParams(vmem_limit_bytes=8 * 1024 * 1024),
    )(*[pltpu.with_memory_space_constraint(piece, pltpu.VMEM) for piece in results])
    dg = dg.T
    if heads > real:
        y = y[:, : real * HEAD_DIM]
        dx = dx[:, : real * HEAD_DIM]
        dg = dg[:, :real]
    return (y, dx, db, dc, dg)


def solution(mesh):
    in_specs = (
        P(("grp", "ctx"), "head"),
        P(("grp", "ctx"), None),
        P(("grp", "ctx"), None),
        P(("grp", "ctx"), "head"),
        P(("grp", "ctx"), "head"),
    )
    out_specs = (
        P(("grp", "ctx"), "head"),
        P(("grp", "ctx"), "head"),
        P(("grp", "ctx"), None),
        P(("grp", "ctx"), None),
        P(("grp", "ctx"), "head"),
    )
    return jax.shard_map(
        functools.partial(per_device, mesh.shape["ctx"], mesh.shape["head"] // 2),
        mesh=mesh,
        in_specs=in_specs,
        out_specs=out_specs,
        check_vma=False,
    )
```

```python
import functools
import math

import jax
import jax.numpy as jnp
from jax import lax
from jax.experimental import pallas as pl
from jax.experimental.pallas import tpu as pltpu
from jax.sharding import PartitionSpec as P

HEAD_DIM = 64
STATE = 128
BLOCK = 256
LANES = 128
FIRST_UNITS = 2
HOP_UNITS = 5
PAIR_TICKS = (4,)
EARLY_TICKS = (1, 1)
MIDDLE_TICKS = 1
CHUNKS = 8
SLABS = 4
STORES = 1
LOG2E = math.log2(math.e)
F32 = jnp.float32
BF16 = jnp.bfloat16
MESH = pl.DeviceIdType.MESH


def mxu(left, right, contract=((1,), (0,))):
    return lax.dot_general(left, right, (contract, ((), ())), preferred_element_type=F32)


def thirds(values):
    high = values.astype(BF16)
    rest = values - high.astype(F32)
    middle = rest.astype(BF16)
    low = (rest - middle.astype(F32)).astype(BF16)
    return jnp.concatenate([high, middle, low], axis=0)


def iota(shape, dim):
    return lax.broadcasted_iota(jnp.int32, shape, dim)


def mixer_kernel(
    ring, chips, heads, blocks,
    x_hbm, b_hbm, c_hbm, ld_hbm, dy_hbm,
    rounded_out, grads, back_in, dg_ref,
    vec, coef, coef_t, ld_in, ldp, runc, runr, scale, gain, scaled, scaled_t, pieces, states, held,
    dev, inc, out_state, inner, scores, ptotal, both, left_w, right_w, bal, mate_in, far_in,
    load_sem,
    chain_send, chain_recv, mate_send, mate_recv, far_send, far_recv, back_send, back_recv,
):
    place = lax.axis_index("ctx")
    head = lax.axis_index("head")
    core = lax.rem(head, 2)
    mate = head + 1 - 2 * core
    chip = lax.div(head, 2)
    pairs = heads // 2
    width = heads * HEAD_DIM
    half = BLOCK // 2
    chunk_rows = STATE // CHUNKS
    slab_rows = STATE // SLABS
    part_rows = slab_rows // 2

    first = (2 * place > ring - 1).astype(jnp.int32)
    second = 1 - first

    loads = [
        pltpu.make_async_copy(ld_hbm, ld_in, load_sem.at[0]),
        pltpu.make_async_copy(c_hbm, coef.at[0], load_sem.at[1]),
        pltpu.make_async_copy(b_hbm, coef.at[1], load_sem.at[2]),
        pltpu.make_async_copy(dy_hbm, vec.at[0], load_sem.at[3]),
        pltpu.make_async_copy(x_hbm, vec.at[1], load_sem.at[4]),
    ]
    loads[0].start()

    @pl.when(first == 0)
    def _():
        for n in (2, 4, 1, 3):
            loads[n].start()

    @pl.when(first == 1)
    def _():
        for n in (1, 3, 2, 4):
            loads[n].start()

    def loaded(v):
        for rest in (coef, vec):
            whole = rest.at[v]
            offset = 1 if rest is coef else 3
            pltpu.make_async_copy(whole, whole, load_sem.at[offset + v]).wait()

    barrier = pltpu.get_barrier_semaphore()
    pl.semaphore_signal(barrier, inc=1, device_id={"head": mate}, device_id_type=MESH)
    for hop in range(1, chips):
        pl.semaphore_signal(
            barrier, inc=1, device_id={"head": lax.rem(head + 2 * hop, 2 * chips)}, device_id_type=MESH
        )

    @pl.when(place > 0)
    def _():
        pl.semaphore_signal(barrier, inc=1, device_id={"ctx": place - 1}, device_id_type=MESH)

    @pl.when(place < ring - 1)
    def _():
        pl.semaphore_signal(barrier, inc=1, device_id={"ctx": place + 1}, device_id_type=MESH)

    slots = ldp.shape[0]
    upper = (iota((BLOCK, BLOCK), 0) <= iota((BLOCK, BLOCK), 1)).astype(F32).astype(BF16)
    spread = (iota((slots, width), 0) == lax.div(iota((slots, width), 1), HEAD_DIM)).astype(F32)
    spread3 = jnp.concatenate([spread] * 3, axis=0).astype(BF16)

    def joined(left3, right):
        three = mxu(left3, right)
        return three[0:slots] + three[slots : 2 * slots] + three[2 * slots :]

    ldp[...] = jnp.zeros_like(ldp)
    loads[0].wait()
    ldp[0:heads, :] = ld_in[...]

    def expanded(values):
        return mxu(thirds(jnp.exp2(values)), spread3, ((0,), (0,)))

    def scaled_pieces(v):
        for j in range(blocks):
            run = runr[j]
            rows = slice(j * BLOCK, (j + 1) * BLOCK)
            scale[v, rows, :] = expanded(jnp.where(v == 0, run, run[:, BLOCK - 1 :] - run))
        loaded(v)
        for j in range(blocks):
            rows = slice(j * BLOCK, (j + 1) * BLOCK)
            flipped = coef[v, rows, :].T
            coef_t[v, j] = flipped
            row = (vec[v, rows, :].astype(F32) * scale[v, rows, :]).astype(BF16)
            scaled[v, rows, :] = row
            pieces[1 - v, j] = mxu(flipped, row)

    for j in range(blocks):
        rows = slice(j * BLOCK, (j + 1) * BLOCK)
        run = joined(thirds(ldp[:, rows]), upper) * LOG2E
        runr[j] = run
        gain[j] = expanded(jnp.broadcast_to(run[:, BLOCK - 1 :], (slots, 8)))

    scaled_pieces(second)

    product = gain[0]
    for j in range(1, blocks):
        product = product * gain[j]
    gain[blocks] = product

    pl.semaphore_wait(barrier, chips + (place > 0).astype(jnp.int32) + (place < ring - 1).astype(jnp.int32))

    def hops(d):
        return jnp.where(d == 0, place, ring - 1 - place)

    def chunk(k):
        return pl.ds(pl.multiple_of(k * chunk_rows, chunk_rows), chunk_rows)

    class Null:
        def start(self): pass
        def wait_recv(self): pass
        def wait_send(self): pass

    class Null:
        def start(self): pass
        def wait_recv(self): pass
        def wait_send(self): pass

    class Null:
        def start(self): pass
        def wait_recv(self): pass
        def wait_send(self): pass

    class Null:
        def start(self): pass
        def wait_recv(self): pass
        def wait_send(self): pass

    class Null:
        def start(self): pass
        def wait_recv(self): pass
        def wait_send(self): pass

    def chain_copy(d, k, source):
        target = jnp.where(d == 0, place + 1, place - 1)
        return pltpu.make_async_remote_copy(
            src_ref=source.at[d, chunk(k)],
            dst_ref=inc.at[d, chunk(k)],
            send_sem=chain_send.at[d],
            recv_sem=chain_recv.at[d, k],
            device_id={"ctx": jnp.clip(target, 0, ring - 1)},
            device_id_type=MESH,
        )

    def device_state(d, sends):
        @pl.loop(0, CHUNKS)
        def _(k):
            at = chunk(k)
            state = pieces[d, jnp.where(d == 0, 0, blocks - 1), at, :]
            for i in range(1, blocks):
                j = jnp.where(d == 0, i, blocks - 1 - i)
                state = gain[j, 0:1, :] * state + pieces[d, j, at, :]
            dev[d, at] = state
            if sends:

                @pl.when(hops(d) == 0)
                def _():
                    inc[d, at] = jnp.zeros((chunk_rows, width), F32)
                    if ring > 1:
                        chain_copy(d, k, dev).start()

    device_state(first, True)
    scaled_pieces(first)
    corner = iota((half, half), 0) >= iota((half, half), 1)
    early, late = slice(0, half), slice(half, BLOCK)
    for j in range(blocks):
        full = mxu(coef[0, j * BLOCK : (j + 1) * BLOCK, :], coef_t[1, j])
        scores[j, 0] = jnp.where(corner, full[early, early], 0.0)
        scores[j, 1] = full[late, early]
        scores[j, 2] = jnp.where(corner, full[late, late], 0.0)
        runc[j] = jnp.concatenate([runr[j], jnp.zeros((LANES - slots, BLOCK), F32)], axis=0).T
    device_state(second, ring == 1)

    def relay(d, k):
        at = chunk(k)
        chain_copy(d, k, out_state).wait_recv()
        out_state[d, at] = gain[blocks, 0:1, :] * inc[d, at] + dev[d, at]
        chain_copy(d, k, out_state).start()

    def passing(d):
        return (hops(d) > 0) & (hops(d) < ring - 1)

    starts = [(d, jnp.where(passing(d), (FIRST_UNITS + HOP_UNITS * (hops(d) - 1)), 1 << 20)) for d in (first, second)]

    def tick(unit):
        for d, start in starts:

            @pl.when((unit >= start) & (unit < start + CHUNKS))
            def _():
                relay(d, unit - start)

    def ticked(unit, target):
        last = jnp.maximum(unit, target)

        @pl.loop(unit, last)
        def _(u):
            tick(u)

        return last

    per_slab = CHUNKS // SLABS

    def needed(d, count):
        return jnp.where(passing(d), (FIRST_UNITS + HOP_UNITS * (hops(d) - 1)) + count, 0)

    def arrive(d, k, count):
        @pl.when((hops(d) > 0) & (hops(d) == ring - 1))
        def _():
            for n in range(count):
                chain_copy(d, k + n, out_state).wait_recv()

    low_lanes = iota((1, LANES), 1) < HEAD_DIM

    def stacked(x2, at):
        zero = jnp.zeros_like(x2[at])
        return jnp.concatenate(
            [jnp.where(low_lanes, x2[at], zero), jnp.where(low_lanes, zero, x2[at])], axis=0
        )


    @pl.loop(0, blocks)
    def _(j):
        rows = pl.ds(pl.multiple_of(j * BLOCK, BLOCK), BLOCK)
        for p in range(pairs):
            lanes = slice(p * LANES, (p + 1) * LANES)
            x2 = vec[1, rows, lanes]
            dy2 = vec[0, rows, lanes]
            pair_left = mxu(dy2, stacked(x2, early), ((1,), (1,)))
            pair_right = mxu(dy2[late], stacked(x2, late), ((1,), (1,)))
            sums = [None] * 3
            for k in range(2):
                h = 2 * p + k
                side = slice(k * half, (k + 1) * half)
                down = runc[j, :, h : h + 1]
                along = runr[j, h : h + 1, :]
                for q, (t, s) in enumerate(((early, early), (late, early), (late, late))):
                    gap = down[t] - along[:, s]
                    decays = jnp.exp2(gap if q == 1 else jnp.minimum(gap, 0.0))
                    weights = (scores[j, q] * decays).astype(BF16)
                    if q < 2:
                        left_w[j, p, t, side] = weights
                        pair = pair_left[t, side] * decays
                    else:
                        right_w[j, p, :, side] = weights
                        pair = pair_right[:, side] * decays
                    sums[q] = pair if k == 0 else sums[q] + pair
            for q in range(3):
                if p == 0:
                    ptotal[q] = sums[q]
                else:
                    ptotal[q] += sums[q]
            for d in range(2):
                scaled_t[d, j, lanes, :] = scaled[d, rows, lanes].T
            if p in PAIR_TICKS:
                tick(j * len(PAIR_TICKS) + PAIR_TICKS.index(p))
        top = jnp.where(corner, ptotal[0], 0.0).astype(BF16)
        bottom = jnp.where(corner, ptotal[2], 0.0).astype(BF16)
        both[j] = jnp.concatenate(
            [
                jnp.concatenate([top, jnp.zeros_like(top)], axis=1),
                jnp.concatenate([ptotal[1].astype(BF16), bottom], axis=1),
            ],
            axis=0,
        )

    for j in range(blocks):
        read_part = mxu(coef_t[1, j], both[j], ((1,), (1,)))
        write_part = mxu(coef_t[0, j], both[j])
        for c in range(SLABS):
            for part in range(2):
                at = (2 * c + part) * part_rows
                grads[0, c, part, j] = read_part[at : at + part_rows]
                grads[1, c, part, j] = write_part[at : at + part_rows]

    def inner_rows(j):
        rows = pl.ds(pl.multiple_of(j * BLOCK, BLOCK), BLOCK)
        for p in range(pairs):
            lanes = slice(p * LANES, (p + 1) * LANES)
            x2 = vec[1, rows, lanes]
            flipped = vec[0, rows, lanes].T
            y_left = mxu(left_w[j, p], stacked(x2, early))
            y_right = mxu(right_w[j, p], stacked(x2, late))
            inner[0, rows, lanes] = jnp.concatenate([y_left[early], y_left[late] + y_right], axis=0)
            dx_early = mxu(flipped, left_w[j, p])
            dx_late = mxu(flipped[:, late], right_w[j, p])
            low, high = slice(0, HEAD_DIM), slice(HEAD_DIM, LANES)
            dx2 = jnp.concatenate(
                [
                    jnp.concatenate([dx_early[low, early], dx_late[low, early]], axis=1),
                    jnp.concatenate([dx_early[high, late], dx_late[high, late]], axis=1),
                ],
                axis=0,
            )
            inner[1, rows, lanes] = dx2.T

    def mate_copy(d, c):
        return pltpu.make_async_remote_copy(
            src_ref=grads.at[d, c, 1 - core],
            dst_ref=mate_in.at[d, c],
            send_sem=mate_send.at[d],
            recv_sem=mate_recv.at[d, c],
            device_id={"head": mate},
            device_id_type=MESH,
        )

    def far_copy(d, c, hop, source):
        return pltpu.make_async_remote_copy(
            src_ref=mate_in.at[d, c],
            dst_ref=far_in.at[d, c, source],
            send_sem=far_send.at[d, hop],
            recv_sem=far_recv.at[d, c, source],
            device_id={"head": lax.rem(head + 2 * hop, 2 * chips)},
            device_id_type=MESH,
        )

    def back_copy(d, c):
        return pltpu.make_async_remote_copy(
            src_ref=grads.at[d, c, core],
            dst_ref=back_in.at[d, c],
            send_sem=back_send.at[d],
            recv_sem=back_recv.at[d],
            device_id={"head": mate},
            device_id_type=MESH,
        )

    def local_sum(d, c):
        mate_copy(d, c).wait_recv()
        total = mate_in[d, c] + grads[d, c, core]
        mate_in[d, c] = total
        for hop in range(1, chips):
            far_copy(d, c, hop, chip).start()
        far_in[d, c, chip] = total

    def far_sum(d, c):
        for hop in range(1, chips):
            far_copy(d, c, hop, lax.rem(chip + chips - hop, chips)).wait_recv()
        total = far_in[d, c, 0]
        for source in range(1, chips):
            total = total + far_in[d, c, source]
        grads[d, c, core] = total
        back_copy(d, c).start()

    def order(d, i):
        return jnp.where(d == 0, i, blocks - 1 - i)

    def outer_part(d, c, offset, count):
        slab = pl.ds(pl.multiple_of(c * slab_rows + offset, part_rows), count)
        now = inc[d, slab]
        for i in range(blocks):
            j = order(d, i)
            states[d, j, slab] = now
            now_held = now.astype(BF16)
            held[d, j, slab] = now_held
            add = mxu(now_held, scaled_t[d, j])
            for n in range(count // part_rows):
                part = offset // part_rows + n
                grads[d, c, part, j] += add[n * part_rows : (n + 1) * part_rows]
            now = gain[j, 0:1, :] * now + pieces[d, j, slab]
        states[d, blocks, slab] = now

    def outer_grads(d, c):
        outer_part(d, c, 0, slab_rows)
        mate_copy(d, c).start()

    pick = (lax.div(iota((width, LANES), 0), HEAD_DIM) == iota((width, LANES), 1)).astype(F32).astype(BF16)

    def outer_rows(d, j, begins):
        other = 1 - d
        rows = pl.ds(pl.multiple_of(j * BLOCK, BLOCK), BLOCK)
        full = inner[d, rows, :] + scale[d, rows, :] * mxu(coef[d, rows, :], held[d, j])
        rounded_out[d, rows, :] = full.astype(BF16)
        term = vec[d, rows, :].astype(F32) * full
        if begins:
            inner[d, rows, :] = term
            return
        term = term - inner[other, rows, :]
        high = term.astype(BF16)
        low = (term - high.astype(F32)).astype(BF16)
        summed = mxu(high, pick) + mxu(low, pick)
        bal[j] = jnp.where(d == 0, summed, -summed)

    def early_step(i, unit):
        unit = ticked(unit, needed(first, (i + 1) * per_slab))
        arrive(first, i * per_slab, per_slab)
        outer_grads(first, i)

        @pl.when(i > 0)
        def _():
            local_sum(first, i - 1)

        unit = ticked(unit, unit + EARLY_TICKS[0])
        inner_rows(i)
        return ticked(unit, unit + EARLY_TICKS[1])

    def late_step(c, unit):
        last = c == SLABS - 1
        unit = ticked(unit, unit + MIDDLE_TICKS)
        unit = ticked(unit, jnp.where(last, 0, needed(second, (c + 1) * per_slab)))

        @pl.when(jnp.logical_not(last))
        def _():
            arrive(second, c * per_slab, per_slab)
            outer_grads(second, c)

        @pl.when(jnp.logical_not(last))
        def _():
            local_sum(jnp.where(c > 0, second, first), jnp.where(c > 0, c - 1, SLABS - 1))

        outer_rows(first, c, True)
        return unit

    unit = lax.fori_loop(0, SLABS, early_step, jnp.int32(blocks * len(PAIR_TICKS)))
    unit = lax.fori_loop(0, SLABS, late_step, unit)
    final = SLABS - 1
    for part in range(2):
        begin = final * per_slab + part * (per_slab // 2)
        unit = ticked(unit, needed(second, begin + per_slab // 2))
        arrive(second, begin, per_slab // 2)
        outer_part(second, final, part * part_rows, part_rows)

        @pl.when(core == 1 - part)
        def _():
            mate_copy(second, final).start()

        if part == 0:
            local_sum(second, final - 1)

    @pl.when(core == 0)
    def _():
        local_sum(second, final)

    outer_rows(second, order(second, 0), False)

    @pl.when(core == 1)
    def _():
        local_sum(second, final)

    @pl.loop(1, blocks)
    def _(i):
        outer_rows(second, order(second, i), False)

    @pl.loop(0, SLABS)
    def _(c):
        far_sum(first, c)

    for j in range(blocks):
        joint = jnp.sum(states[0, j + 1] * states[1, j], axis=0, keepdims=True)
        later = jnp.sum(spread * joint, axis=1, keepdims=True)
        lower = (iota((BLOCK, BLOCK), 0) >= iota((BLOCK, BLOCK), 1)).astype(F32).astype(BF16)
        suffix = joined(thirds(bal[j].T[0:slots]), lower) + later
        dg_ref[:, j * BLOCK : (j + 1) * BLOCK] = suffix[0:heads, :]

    @pl.loop(0, SLABS)
    def _(c):
        far_sum(second, c)

    def whole(d, source, target, send, recv):
        return pltpu.make_async_remote_copy(
            src_ref=source.at[d],
            dst_ref=target.at[d],
            send_sem=send,
            recv_sem=recv,
            device_id={"head": mate},
            device_id_type=MESH,
        )

    for d in range(2):
        everything = whole(d, mate_in, back_in, back_send.at[d], back_recv.at[d])
        everything.wait_recv()
        everything.wait_send()
        whole(d, mate_in, back_in, mate_send.at[d], back_recv.at[d]).wait_send()
        for hop in range(1, chips):
            whole(d, mate_in, back_in, far_send.at[d, hop], back_recv.at[d]).wait_send()

        @pl.when(hops(d) < ring - 1)
        def _():
            whole(d, out_state, inc, chain_send.at[d], back_recv.at[d]).wait_send()


def store_kernel(rounded_out, grads, back_in, dg_in, y_hbm, dx_hbm, db_hbm, dc_hbm, dg_hbm, turned, sem):
    core = lax.rem(lax.axis_index("head"), 2)
    copies = [pltpu.make_async_copy(dg_in, dg_hbm, sem.at[0])]
    tokens = rounded_out.shape[1]
    for part in range(STORES):
        rows = pl.ds(part * (tokens // STORES), tokens // STORES)
        for d, out in ((0, y_hbm), (1, dx_hbm)):
            copies.append(
                pltpu.make_async_copy(rounded_out.at[d, rows], out.at[rows], sem.at[len(copies)])
            )
    for copy in copies:
        copy.start()
    for d, out in ((0, dc_hbm), (1, db_hbm)):
        for j in range(grads.shape[3]):
            parts = []
            for c in range(SLABS):
                own, other = grads[d, c, core, j], back_in[d, c, j]
                parts += [jnp.where(core == 0, own, other), jnp.where(core == 0, other, own)]
            turned[d, j * BLOCK : (j + 1) * BLOCK, :] = jnp.concatenate(parts, axis=0).T
        copies.append(pltpu.make_async_copy(turned.at[d], out, sem.at[len(copies)]))
        copies[-1].start()
    for copy in copies:
        copy.wait()


def hbm(array):
    return pltpu.with_memory_space_constraint(array, pltpu.HBM)


def per_device(ring, chips, inputs, write_coeffs, read_coeffs, log_decay, out_grad):
    tokens = inputs.shape[0]
    real = log_decay.shape[1]
    heads = real + real % 2
    if heads > real:
        extra = ((0, 0), (0, (heads - real) * HEAD_DIM))
        inputs = jnp.pad(inputs, extra)
        out_grad = jnp.pad(out_grad, extra)
        log_decay = jnp.pad(log_decay, ((0, 0), (0, heads - real)))
    width = heads * HEAD_DIM
    blocks = tokens // BLOCK
    pairs = heads // 2
    half = BLOCK // 2
    part_rows = STATE // SLABS // 2
    slots = -(-heads // 16) * 16
    any_spec = pl.BlockSpec(memory_space=pl.ANY)
    hbm_spec = pl.BlockSpec(memory_space=pltpu.HBM)
    vmem_spec = pl.BlockSpec(memory_space=pltpu.VMEM)
    dma = pltpu.SemaphoreType.DMA
    results = pl.pallas_call(
        functools.partial(mixer_kernel, ring, chips, heads, blocks),
        out_shape=(
            pltpu.VMEM((2, tokens, width), BF16),
            pltpu.VMEM((2, SLABS, 2, blocks, part_rows, BLOCK), F32),
            pltpu.VMEM((2, SLABS, blocks, part_rows, BLOCK), F32),
            pltpu.VMEM((heads, tokens), F32),
        ),
        in_specs=[hbm_spec] * 5,
        out_specs=(vmem_spec,) * 4,
        scratch_shapes=[
            pltpu.VMEM((2, tokens, width), BF16),
            pltpu.VMEM((2, tokens, STATE), BF16),
            pltpu.VMEM((2, blocks, STATE, BLOCK), BF16),
            pltpu.VMEM((heads, tokens), F32),
            pltpu.VMEM((slots, tokens), F32),
            pltpu.VMEM((blocks, BLOCK, LANES), F32),
            pltpu.VMEM((blocks, slots, BLOCK), F32),
            pltpu.VMEM((2, tokens, width), F32),
            pltpu.VMEM((blocks + 1, 8, width), F32),
            pltpu.VMEM((2, tokens, width), BF16),
            pltpu.VMEM((2, blocks, width, BLOCK), BF16),
            pltpu.VMEM((2, blocks, STATE, width), F32),
            pltpu.VMEM((2, blocks + 1, STATE, width), F32),
            pltpu.VMEM((2, blocks, STATE, width), BF16),
            pltpu.VMEM((2, STATE, width), F32),
            pltpu.VMEM((2, STATE, width), F32),
            pltpu.VMEM((2, STATE, width), F32),
            pltpu.VMEM((2, tokens, width), F32),
            pltpu.VMEM((blocks, 3, half, half), F32),
            pltpu.VMEM((3, half, half), F32),
            pltpu.VMEM((blocks, BLOCK, BLOCK), BF16),
            pltpu.VMEM((blocks, pairs, BLOCK, BLOCK), BF16),
            pltpu.VMEM((blocks, pairs, half, BLOCK), BF16),
            pltpu.VMEM((blocks, BLOCK, LANES), F32),
            pltpu.VMEM((2, SLABS, blocks, part_rows, BLOCK), F32),
            pltpu.VMEM((2, SLABS, chips, blocks, part_rows, BLOCK), F32),
            dma((5,)),
            dma((2,)),
            dma((2, CHUNKS)),
            dma((2,)),
            dma((2, SLABS)),
            dma((2, chips)),
            dma((2, SLABS, chips)),
            dma((2,)),
            dma((2,)),
        ],
        compiler_params=pltpu.CompilerParams(
            collective_id=0, has_side_effects=True, vmem_limit_bytes=46 * 1024 * 1024
        ),
    )(hbm(inputs), hbm(write_coeffs), hbm(read_coeffs), hbm(log_decay.T), hbm(out_grad))
    y, dx, db, dc, dg = pl.pallas_call(
        store_kernel,
        out_shape=(
            jax.ShapeDtypeStruct((tokens, width), BF16),
            jax.ShapeDtypeStruct((tokens, width), BF16),
            jax.ShapeDtypeStruct((tokens, STATE), F32),
            jax.ShapeDtypeStruct((tokens, STATE), F32),
            jax.ShapeDtypeStruct((heads, tokens), F32),
        ),
        in_specs=[vmem_spec] * 4,
        out_specs=(any_spec,) * 5,
        scratch_shapes=[pltpu.VMEM((2, tokens, STATE), F32), dma((3 + 2 * STORES,))],
        compiler_params=pltpu.CompilerParams(vmem_limit_bytes=8 * 1024 * 1024),
    )(*[pltpu.with_memory_space_constraint(piece, pltpu.VMEM) for piece in results])
    dg = dg.T
    if heads > real:
        y = y[:, : real * HEAD_DIM]
        dx = dx[:, : real * HEAD_DIM]
        dg = dg[:, :real]
    return (y, dx, db, dc, dg)


def solution(mesh):
    in_specs = (
        P(("grp", "ctx"), "head"),
        P(("grp", "ctx"), None),
        P(("grp", "ctx"), None),
        P(("grp", "ctx"), "head"),
        P(("grp", "ctx"), "head"),
    )
    out_specs = (
        P(("grp", "ctx"), "head"),
        P(("grp", "ctx"), "head"),
        P(("grp", "ctx"), None),
        P(("grp", "ctx"), None),
        P(("grp", "ctx"), "head"),
    )
    return jax.shard_map(
        functools.partial(per_device, mesh.shape["ctx"], mesh.shape["head"] // 2),
        mesh=mesh,
        in_specs=in_specs,
        out_specs=out_specs,
        check_vma=False,
    )
```

```python
import functools
import math

import jax
import jax.numpy as jnp
from jax import lax
from jax.experimental import pallas as pl
from jax.experimental.pallas import tpu as pltpu
from jax.sharding import PartitionSpec as P

HEAD_DIM = 64
STATE = 128
BLOCK = 256
LANES = 128
FIRST_UNITS = 2
HOP_UNITS = 5
EARLY_TICKS = (1, 1)
MIDDLE_TICKS = 1
CHUNKS = 8
SLABS = 4
STORES = 1
LOG2E = math.log2(math.e)
F32 = jnp.float32
BF16 = jnp.bfloat16
MESH = pl.DeviceIdType.MESH


def mxu(left, right, contract=((1,), (0,))):
    return lax.dot_general(left, right, (contract, ((), ())), preferred_element_type=F32)


def thirds(values):
    high = values.astype(BF16)
    rest = values - high.astype(F32)
    middle = rest.astype(BF16)
    low = (rest - middle.astype(F32)).astype(BF16)
    return jnp.concatenate([high, middle, low], axis=0)


def iota(shape, dim):
    return lax.broadcasted_iota(jnp.int32, shape, dim)


def mixer_kernel(
    ring, chips, heads, blocks,
    x_hbm, b_hbm, c_hbm, ld_hbm, dy_hbm,
    rounded_out, grads, back_in, dg_ref,
    vec, coef, coef_t, ld_in, ldp, runc, runr, scale, gain, scaled, scaled_t, pieces, states, held,
    dev, inc, out_state, inner, scores, ptotal, both, left_w, right_w, bal, mate_in, far_in,
    load_sem,
    chain_send, chain_recv, mate_send, mate_recv, far_send, far_recv, back_send, back_recv,
):
    place = lax.axis_index("ctx")
    head = lax.axis_index("head")
    core = lax.rem(head, 2)
    mate = head + 1 - 2 * core
    chip = lax.div(head, 2)
    pairs = heads // 2
    width = heads * HEAD_DIM
    half = BLOCK // 2
    chunk_rows = STATE // CHUNKS
    slab_rows = STATE // SLABS
    part_rows = slab_rows // 2

    first = (2 * place > ring - 1).astype(jnp.int32)
    second = 1 - first

    loads = [
        pltpu.make_async_copy(ld_hbm, ld_in, load_sem.at[0]),
        pltpu.make_async_copy(c_hbm, coef.at[0], load_sem.at[1]),
        pltpu.make_async_copy(b_hbm, coef.at[1], load_sem.at[2]),
        pltpu.make_async_copy(dy_hbm, vec.at[0], load_sem.at[3]),
        pltpu.make_async_copy(x_hbm, vec.at[1], load_sem.at[4]),
    ]
    loads[0].start()

    @pl.when(first == 0)
    def _():
        for n in (2, 4, 1, 3):
            loads[n].start()

    @pl.when(first == 1)
    def _():
        for n in (1, 3, 2, 4):
            loads[n].start()

    def loaded(v):
        for rest in (coef, vec):
            whole = rest.at[v]
            offset = 1 if rest is coef else 3
            pltpu.make_async_copy(whole, whole, load_sem.at[offset + v]).wait()

    barrier = pltpu.get_barrier_semaphore()
    pl.semaphore_signal(barrier, inc=1, device_id={"head": mate}, device_id_type=MESH)
    for hop in range(1, chips):
        pl.semaphore_signal(
            barrier, inc=1, device_id={"head": lax.rem(head + 2 * hop, 2 * chips)}, device_id_type=MESH
        )

    @pl.when(place > 0)
    def _():
        pl.semaphore_signal(barrier, inc=1, device_id={"ctx": place - 1}, device_id_type=MESH)

    @pl.when(place < ring - 1)
    def _():
        pl.semaphore_signal(barrier, inc=1, device_id={"ctx": place + 1}, device_id_type=MESH)

    slots = ldp.shape[0]
    upper = (iota((BLOCK, BLOCK), 0) <= iota((BLOCK, BLOCK), 1)).astype(F32).astype(BF16)
    spread = (iota((slots, width), 0) == lax.div(iota((slots, width), 1), HEAD_DIM)).astype(F32)
    spread3 = jnp.concatenate([spread] * 3, axis=0).astype(BF16)

    def joined(left3, right):
        three = mxu(left3, right)
        return three[0:slots] + three[slots : 2 * slots] + three[2 * slots :]

    ldp[...] = jnp.zeros_like(ldp)
    loads[0].wait()
    ldp[0:heads, :] = ld_in[...]

    def expanded(values):
        return mxu(thirds(jnp.exp2(values)), spread3, ((0,), (0,)))

    def scaled_pieces(v):
        for j in range(blocks):
            run = runr[j]
            rows = slice(j * BLOCK, (j + 1) * BLOCK)
            scale[v, rows, :] = expanded(jnp.where(v == 0, run, run[:, BLOCK - 1 :] - run))
        loaded(v)
        for j in range(blocks):
            rows = slice(j * BLOCK, (j + 1) * BLOCK)
            flipped = coef[v, rows, :].T
            coef_t[v, j] = flipped
            row = (vec[v, rows, :].astype(F32) * scale[v, rows, :]).astype(BF16)
            scaled[v, rows, :] = row
            pieces[1 - v, j] = mxu(flipped, row)

    for j in range(blocks):
        rows = slice(j * BLOCK, (j + 1) * BLOCK)
        run = joined(thirds(ldp[:, rows]), upper) * LOG2E
        runr[j] = run
        gain[j] = expanded(jnp.broadcast_to(run[:, BLOCK - 1 :], (slots, 8)))

    scaled_pieces(second)

    product = gain[0]
    for j in range(1, blocks):
        product = product * gain[j]
    gain[blocks] = product

    pl.semaphore_wait(barrier, chips + (place > 0).astype(jnp.int32) + (place < ring - 1).astype(jnp.int32))

    def hops(d):
        return jnp.where(d == 0, place, ring - 1 - place)

    def chunk(k):
        return pl.ds(pl.multiple_of(k * chunk_rows, chunk_rows), chunk_rows)

    class Null:
        def start(self): pass
        def wait_recv(self): pass
        def wait_send(self): pass

    class Null:
        def start(self): pass
        def wait_recv(self): pass
        def wait_send(self): pass

    class Null:
        def start(self): pass
        def wait_recv(self): pass
        def wait_send(self): pass

    class Null:
        def start(self): pass
        def wait_recv(self): pass
        def wait_send(self): pass

    class Null:
        def start(self): pass
        def wait_recv(self): pass
        def wait_send(self): pass

    def chain_copy(d, k, source):
        target = jnp.where(d == 0, place + 1, place - 1)
        return pltpu.make_async_remote_copy(
            src_ref=source.at[d, chunk(k)],
            dst_ref=inc.at[d, chunk(k)],
            send_sem=chain_send.at[d],
            recv_sem=chain_recv.at[d, k],
            device_id={"ctx": jnp.clip(target, 0, ring - 1)},
            device_id_type=MESH,
        )

    def device_state(d, sends):
        @pl.loop(0, CHUNKS)
        def _(k):
            at = chunk(k)
            state = pieces[d, jnp.where(d == 0, 0, blocks - 1), at, :]
            for i in range(1, blocks):
                j = jnp.where(d == 0, i, blocks - 1 - i)
                state = gain[j, 0:1, :] * state + pieces[d, j, at, :]
            dev[d, at] = state
            if sends:

                @pl.when(hops(d) == 0)
                def _():
                    inc[d, at] = jnp.zeros((chunk_rows, width), F32)
                    if ring > 1:
                        chain_copy(d, k, dev).start()

    device_state(first, True)
    scaled_pieces(first)
    corner = iota((half, half), 0) >= iota((half, half), 1)
    early, late = slice(0, half), slice(half, BLOCK)
    for j in range(blocks):
        full = mxu(coef[0, j * BLOCK : (j + 1) * BLOCK, :], coef_t[1, j])
        scores[j, 0] = jnp.where(corner, full[early, early], 0.0)
        scores[j, 1] = full[late, early]
        scores[j, 2] = jnp.where(corner, full[late, late], 0.0)
        runc[j] = jnp.concatenate([runr[j], jnp.zeros((LANES - slots, BLOCK), F32)], axis=0).T
    device_state(second, ring == 1)

    def relay(d, k):
        at = chunk(k)
        chain_copy(d, k, out_state).wait_recv()
        out_state[d, at] = gain[blocks, 0:1, :] * inc[d, at] + dev[d, at]
        chain_copy(d, k, out_state).start()

    def passing(d):
        return (hops(d) > 0) & (hops(d) < ring - 1)

    starts = [(d, jnp.where(passing(d), (FIRST_UNITS + HOP_UNITS * (hops(d) - 1)), 1 << 20)) for d in (first, second)]

    def tick(unit):
        for d, start in starts:

            @pl.when((unit >= start) & (unit < start + CHUNKS))
            def _():
                relay(d, unit - start)

    def ticked(unit, target):
        last = jnp.maximum(unit, target)

        @pl.loop(unit, last)
        def _(u):
            tick(u)

        return last

    per_slab = CHUNKS // SLABS

    def needed(d, count):
        return jnp.where(passing(d), (FIRST_UNITS + HOP_UNITS * (hops(d) - 1)) + count, 0)

    def arrive(d, k, count):
        @pl.when((hops(d) > 0) & (hops(d) == ring - 1))
        def _():
            for n in range(count):
                chain_copy(d, k + n, out_state).wait_recv()

    low_lanes = iota((1, LANES), 1) < HEAD_DIM

    def stacked(x2, at):
        zero = jnp.zeros_like(x2[at])
        return jnp.concatenate(
            [jnp.where(low_lanes, x2[at], zero), jnp.where(low_lanes, zero, x2[at])], axis=0
        )


    @pl.loop(0, blocks)
    def _(j):
        rows = pl.ds(pl.multiple_of(j * BLOCK, BLOCK), BLOCK)
        for p in range(pairs):
            lanes = slice(p * LANES, (p + 1) * LANES)
            x2 = vec[1, rows, lanes]
            dy2 = vec[0, rows, lanes]
            pair_left = mxu(dy2, stacked(x2, early), ((1,), (1,)))
            pair_right = mxu(dy2[late], stacked(x2, late), ((1,), (1,)))
            sums = [None] * 3
            for k in range(2):
                h = 2 * p + k
                side = slice(k * half, (k + 1) * half)
                down = runc[j, :, h : h + 1]
                along = runr[j, h : h + 1, :]
                for q, (t, s) in enumerate(((early, early), (late, early), (late, late))):
                    gap = down[t] - along[:, s]
                    decays = jnp.exp2(gap if q == 1 else jnp.minimum(gap, 0.0))
                    weights = (scores[j, q] * decays).astype(BF16)
                    if q < 2:
                        left_w[j, p, t, side] = weights
                        pair = pair_left[t, side] * decays
                    else:
                        right_w[j, p, :, side] = weights
                        pair = pair_right[:, side] * decays
                    sums[q] = pair if k == 0 else sums[q] + pair
            for q in range(3):
                if p == 0:
                    ptotal[q] = sums[q]
                else:
                    ptotal[q] += sums[q]
            for d in range(2):
                scaled_t[d, j, lanes, :] = scaled[d, rows, lanes].T
            if p == pairs - 1:
                tick(j)
        top = jnp.where(corner, ptotal[0], 0.0).astype(BF16)
        bottom = jnp.where(corner, ptotal[2], 0.0).astype(BF16)
        both[j] = jnp.concatenate(
            [
                jnp.concatenate([top, jnp.zeros_like(top)], axis=1),
                jnp.concatenate([ptotal[1].astype(BF16), bottom], axis=1),
            ],
            axis=0,
        )

    for j in range(blocks):
        read_part = mxu(coef_t[1, j], both[j], ((1,), (1,)))
        write_part = mxu(coef_t[0, j], both[j])
        for c in range(SLABS):
            for part in range(2):
                at = (2 * c + part) * part_rows
                grads[0, c, part, j] = read_part[at : at + part_rows]
                grads[1, c, part, j] = write_part[at : at + part_rows]

    def inner_rows(j):
        rows = pl.ds(pl.multiple_of(j * BLOCK, BLOCK), BLOCK)
        for p in range(pairs):
            lanes = slice(p * LANES, (p + 1) * LANES)
            x2 = vec[1, rows, lanes]
            flipped = vec[0, rows, lanes].T
            y_left = mxu(left_w[j, p], stacked(x2, early))
            y_right = mxu(right_w[j, p], stacked(x2, late))
            inner[0, rows, lanes] = jnp.concatenate([y_left[early], y_left[late] + y_right], axis=0)
            dx_early = mxu(flipped, left_w[j, p])
            dx_late = mxu(flipped[:, late], right_w[j, p])
            low, high = slice(0, HEAD_DIM), slice(HEAD_DIM, LANES)
            dx2 = jnp.concatenate(
                [
                    jnp.concatenate([dx_early[low, early], dx_late[low, early]], axis=1),
                    jnp.concatenate([dx_early[high, late], dx_late[high, late]], axis=1),
                ],
                axis=0,
            )
            inner[1, rows, lanes] = dx2.T

    def mate_copy(d, c):
        return pltpu.make_async_remote_copy(
            src_ref=grads.at[d, c, 1 - core],
            dst_ref=mate_in.at[d, c],
            send_sem=mate_send.at[d],
            recv_sem=mate_recv.at[d, c],
            device_id={"head": mate},
            device_id_type=MESH,
        )

    def far_copy(d, c, hop, source):
        return pltpu.make_async_remote_copy(
            src_ref=mate_in.at[d, c],
            dst_ref=far_in.at[d, c, source],
            send_sem=far_send.at[d, hop],
            recv_sem=far_recv.at[d, c, source],
            device_id={"head": lax.rem(head + 2 * hop, 2 * chips)},
            device_id_type=MESH,
        )

    def back_copy(d, c):
        return pltpu.make_async_remote_copy(
            src_ref=grads.at[d, c, core],
            dst_ref=back_in.at[d, c],
            send_sem=back_send.at[d],
            recv_sem=back_recv.at[d],
            device_id={"head": mate},
            device_id_type=MESH,
        )

    def local_sum(d, c):
        mate_copy(d, c).wait_recv()
        total = mate_in[d, c] + grads[d, c, core]
        mate_in[d, c] = total
        for hop in range(1, chips):
            far_copy(d, c, hop, chip).start()
        far_in[d, c, chip] = total

    def far_sum(d, c):
        for hop in range(1, chips):
            far_copy(d, c, hop, lax.rem(chip + chips - hop, chips)).wait_recv()
        total = far_in[d, c, 0]
        for source in range(1, chips):
            total = total + far_in[d, c, source]
        grads[d, c, core] = total
        back_copy(d, c).start()

    def order(d, i):
        return jnp.where(d == 0, i, blocks - 1 - i)

    def outer_part(d, c, offset, count):
        slab = pl.ds(pl.multiple_of(c * slab_rows + offset, part_rows), count)
        now = inc[d, slab]
        for i in range(blocks):
            j = order(d, i)
            states[d, j, slab] = now
            now_held = now.astype(BF16)
            held[d, j, slab] = now_held
            add = mxu(now_held, scaled_t[d, j])
            for n in range(count // part_rows):
                part = offset // part_rows + n
                grads[d, c, part, j] += add[n * part_rows : (n + 1) * part_rows]
            now = gain[j, 0:1, :] * now + pieces[d, j, slab]
        states[d, blocks, slab] = now

    def outer_grads(d, c):
        outer_part(d, c, 0, slab_rows)
        mate_copy(d, c).start()

    pick = (lax.div(iota((width, LANES), 0), HEAD_DIM) == iota((width, LANES), 1)).astype(F32).astype(BF16)

    def outer_rows(d, j, begins):
        other = 1 - d
        rows = pl.ds(pl.multiple_of(j * BLOCK, BLOCK), BLOCK)
        full = inner[d, rows, :] + scale[d, rows, :] * mxu(coef[d, rows, :], held[d, j])
        rounded_out[d, rows, :] = full.astype(BF16)
        term = vec[d, rows, :].astype(F32) * full
        if begins:
            inner[d, rows, :] = term
            return
        term = term - inner[other, rows, :]
        high = term.astype(BF16)
        low = (term - high.astype(F32)).astype(BF16)
        summed = mxu(high, pick) + mxu(low, pick)
        bal[j] = jnp.where(d == 0, summed, -summed)

    def early_step(i, unit):
        unit = ticked(unit, needed(first, (i + 1) * per_slab))
        arrive(first, i * per_slab, per_slab)
        outer_grads(first, i)

        @pl.when(i > 0)
        def _():
            local_sum(first, i - 1)

        unit = ticked(unit, unit + EARLY_TICKS[0])
        inner_rows(i)
        return ticked(unit, unit + EARLY_TICKS[1])

    def late_step(c, unit):
        last = c == SLABS - 1
        unit = ticked(unit, unit + MIDDLE_TICKS)
        unit = ticked(unit, jnp.where(last, 0, needed(second, (c + 1) * per_slab)))

        @pl.when(jnp.logical_not(last))
        def _():
            arrive(second, c * per_slab, per_slab)
            outer_grads(second, c)

        @pl.when(jnp.logical_not(last))
        def _():
            local_sum(jnp.where(c > 0, second, first), jnp.where(c > 0, c - 1, SLABS - 1))

        outer_rows(first, c, True)
        return unit

    unit = lax.fori_loop(0, SLABS, early_step, jnp.int32(blocks))
    unit = lax.fori_loop(0, SLABS, late_step, unit)
    final = SLABS - 1
    for part in range(2):
        begin = final * per_slab + part * (per_slab // 2)
        unit = ticked(unit, needed(second, begin + per_slab // 2))
        arrive(second, begin, per_slab // 2)
        outer_part(second, final, part * part_rows, part_rows)

        @pl.when(core == 1 - part)
        def _():
            mate_copy(second, final).start()

        if part == 0:
            local_sum(second, final - 1)

    @pl.when(core == 0)
    def _():
        local_sum(second, final)

    outer_rows(second, order(second, 0), False)

    @pl.when(core == 1)
    def _():
        local_sum(second, final)

    @pl.loop(1, blocks)
    def _(i):
        outer_rows(second, order(second, i), False)

    @pl.loop(0, SLABS)
    def _(c):
        far_sum(first, c)

    for j in range(blocks):
        joint = jnp.sum(states[0, j + 1] * states[1, j], axis=0, keepdims=True)
        later = jnp.sum(spread * joint, axis=1, keepdims=True)
        lower = (iota((BLOCK, BLOCK), 0) >= iota((BLOCK, BLOCK), 1)).astype(F32).astype(BF16)
        suffix = joined(thirds(bal[j].T[0:slots]), lower) + later
        dg_ref[:, j * BLOCK : (j + 1) * BLOCK] = suffix[0:heads, :]

    @pl.loop(0, SLABS)
    def _(c):
        far_sum(second, c)

    def whole(d, source, target, send, recv):
        return pltpu.make_async_remote_copy(
            src_ref=source.at[d],
            dst_ref=target.at[d],
            send_sem=send,
            recv_sem=recv,
            device_id={"head": mate},
            device_id_type=MESH,
        )

    for d in range(2):
        everything = whole(d, mate_in, back_in, back_send.at[d], back_recv.at[d])
        everything.wait_recv()
        everything.wait_send()
        whole(d, mate_in, back_in, mate_send.at[d], back_recv.at[d]).wait_send()
        for hop in range(1, chips):
            whole(d, mate_in, back_in, far_send.at[d, hop], back_recv.at[d]).wait_send()

        @pl.when(hops(d) < ring - 1)
        def _():
            whole(d, out_state, inc, chain_send.at[d], back_recv.at[d]).wait_send()


def store_kernel(rounded_out, grads, back_in, dg_in, y_hbm, dx_hbm, db_hbm, dc_hbm, dg_hbm, turned, sem):
    core = lax.rem(lax.axis_index("head"), 2)
    copies = [pltpu.make_async_copy(dg_in, dg_hbm, sem.at[0])]
    tokens = rounded_out.shape[1]
    for part in range(STORES):
        rows = pl.ds(part * (tokens // STORES), tokens // STORES)
        for d, out in ((0, y_hbm), (1, dx_hbm)):
            copies.append(
                pltpu.make_async_copy(rounded_out.at[d, rows], out.at[rows], sem.at[len(copies)])
            )
    for copy in copies:
        copy.start()
    for d, out in ((0, dc_hbm), (1, db_hbm)):
        for j in range(grads.shape[3]):
            parts = []
            for c in range(SLABS):
                own, other = grads[d, c, core, j], back_in[d, c, j]
                parts += [jnp.where(core == 0, own, other), jnp.where(core == 0, other, own)]
            turned[d, j * BLOCK : (j + 1) * BLOCK, :] = jnp.concatenate(parts, axis=0).T
        copies.append(pltpu.make_async_copy(turned.at[d], out, sem.at[len(copies)]))
        copies[-1].start()
    for copy in copies:
        copy.wait()


def hbm(array):
    return pltpu.with_memory_space_constraint(array, pltpu.HBM)


def per_device(ring, chips, inputs, write_coeffs, read_coeffs, log_decay, out_grad):
    tokens = inputs.shape[0]
    real = log_decay.shape[1]
    heads = real + real % 2
    if heads > real:
        extra = ((0, 0), (0, (heads - real) * HEAD_DIM))
        inputs = jnp.pad(inputs, extra)
        out_grad = jnp.pad(out_grad, extra)
        log_decay = jnp.pad(log_decay, ((0, 0), (0, heads - real)))
    width = heads * HEAD_DIM
    blocks = tokens // BLOCK
    pairs = heads // 2
    half = BLOCK // 2
    part_rows = STATE // SLABS // 2
    slots = -(-heads // 16) * 16
    any_spec = pl.BlockSpec(memory_space=pl.ANY)
    hbm_spec = pl.BlockSpec(memory_space=pltpu.HBM)
    vmem_spec = pl.BlockSpec(memory_space=pltpu.VMEM)
    dma = pltpu.SemaphoreType.DMA
    results = pl.pallas_call(
        functools.partial(mixer_kernel, ring, chips, heads, blocks),
        out_shape=(
            pltpu.VMEM((2, tokens, width), BF16),
            pltpu.VMEM((2, SLABS, 2, blocks, part_rows, BLOCK), F32),
            pltpu.VMEM((2, SLABS, blocks, part_rows, BLOCK), F32),
            pltpu.VMEM((heads, tokens), F32),
        ),
        in_specs=[hbm_spec] * 5,
        out_specs=(vmem_spec,) * 4,
        scratch_shapes=[
            pltpu.VMEM((2, tokens, width), BF16),
            pltpu.VMEM((2, tokens, STATE), BF16),
            pltpu.VMEM((2, blocks, STATE, BLOCK), BF16),
            pltpu.VMEM((heads, tokens), F32),
            pltpu.VMEM((slots, tokens), F32),
            pltpu.VMEM((blocks, BLOCK, LANES), F32),
            pltpu.VMEM((blocks, slots, BLOCK), F32),
            pltpu.VMEM((2, tokens, width), F32),
            pltpu.VMEM((blocks + 1, 8, width), F32),
            pltpu.VMEM((2, tokens, width), BF16),
            pltpu.VMEM((2, blocks, width, BLOCK), BF16),
            pltpu.VMEM((2, blocks, STATE, width), F32),
            pltpu.VMEM((2, blocks + 1, STATE, width), F32),
            pltpu.VMEM((2, blocks, STATE, width), BF16),
            pltpu.VMEM((2, STATE, width), F32),
            pltpu.VMEM((2, STATE, width), F32),
            pltpu.VMEM((2, STATE, width), F32),
            pltpu.VMEM((2, tokens, width), F32),
            pltpu.VMEM((blocks, 3, half, half), F32),
            pltpu.VMEM((3, half, half), F32),
            pltpu.VMEM((blocks, BLOCK, BLOCK), BF16),
            pltpu.VMEM((blocks, pairs, BLOCK, BLOCK), BF16),
            pltpu.VMEM((blocks, pairs, half, BLOCK), BF16),
            pltpu.VMEM((blocks, BLOCK, LANES), F32),
            pltpu.VMEM((2, SLABS, blocks, part_rows, BLOCK), F32),
            pltpu.VMEM((2, SLABS, chips, blocks, part_rows, BLOCK), F32),
            dma((5,)),
            dma((2,)),
            dma((2, CHUNKS)),
            dma((2,)),
            dma((2, SLABS)),
            dma((2, chips)),
            dma((2, SLABS, chips)),
            dma((2,)),
            dma((2,)),
        ],
        compiler_params=pltpu.CompilerParams(
            collective_id=0, has_side_effects=True, vmem_limit_bytes=46 * 1024 * 1024
        ),
    )(hbm(inputs), hbm(write_coeffs), hbm(read_coeffs), hbm(log_decay.T), hbm(out_grad))
    y, dx, db, dc, dg = pl.pallas_call(
        store_kernel,
        out_shape=(
            jax.ShapeDtypeStruct((tokens, width), BF16),
            jax.ShapeDtypeStruct((tokens, width), BF16),
            jax.ShapeDtypeStruct((tokens, STATE), F32),
            jax.ShapeDtypeStruct((tokens, STATE), F32),
            jax.ShapeDtypeStruct((heads, tokens), F32),
        ),
        in_specs=[vmem_spec] * 4,
        out_specs=(any_spec,) * 5,
        scratch_shapes=[pltpu.VMEM((2, tokens, STATE), F32), dma((3 + 2 * STORES,))],
        compiler_params=pltpu.CompilerParams(vmem_limit_bytes=8 * 1024 * 1024),
    )(*[pltpu.with_memory_space_constraint(piece, pltpu.VMEM) for piece in results])
    dg = dg.T
    if heads > real:
        y = y[:, : real * HEAD_DIM]
        dx = dx[:, : real * HEAD_DIM]
        dg = dg[:, :real]
    return (y, dx, db, dc, dg)


def solution(mesh):
    in_specs = (
        P(("grp", "ctx"), "head"),
        P(("grp", "ctx"), None),
        P(("grp", "ctx"), None),
        P(("grp", "ctx"), "head"),
        P(("grp", "ctx"), "head"),
    )
    out_specs = (
        P(("grp", "ctx"), "head"),
        P(("grp", "ctx"), "head"),
        P(("grp", "ctx"), None),
        P(("grp", "ctx"), None),
        P(("grp", "ctx"), "head"),
    )
    return jax.shard_map(
        functools.partial(per_device, mesh.shape["ctx"], mesh.shape["head"] // 2),
        mesh=mesh,
        in_specs=in_specs,
        out_specs=out_specs,
        check_vma=False,
    )
```
